768 devices in a mesh: seq: 48 (over y, z_lo), head: 16 (over z_hi, x, core).
Axes of the slice: x: 4, y: 8, z: 12 (z_hi: 2, z_lo: 6; z = z_hi * 6 + z_lo), core: 2. Of those that a mesh axis runs over, the one named last changes fastest.
Arguments:
- query_rows: bfloat16 [36864, 2048], P('seq', 'head'), may hold values from -6 to 6
- key_rows: bfloat16 [36864, 2048], P('seq', 'head'), may hold values from -6 to 6
- value_rows: bfloat16 [36864, 2048], P('seq', 'head'), may hold values from -6 to 6
- output_rows: bfloat16 [36864, 2048], P('seq', 'head'), may hold values from -6 to 6
- output_grad: bfloat16 [36864, 2048], P('seq', 'head'), may hold values from -6 to 6
- projection: bfloat16 [3, 2048, 3072], P(None, 'head'), may hold values from -0.078125 to 0.078125
- neighbours: int32 [96, 4], replicated, may hold values from 0 to 95, as said below
- counts: int32 [96], replicated, may hold values from 3 to 4, as said below
Outputs:
- input_grad: bfloat16 [36864, 3072], P('seq', 'head')
The draws below stay inside these ranges and needn't reach their ends.
Inputs may be any that keep to these rules, and one draw needn't show every extreme that they name: `neighbours`: row t lists 4 different tiles: first t itself, then t - 1, then t + 1 (modulo 96); the others lie among tiles (t // 2 - 1) * 2 to (t // 2 + 2) * 2 - 1, taken modulo 96. `counts`: every tile uses at least its first three listed tiles; some tile uses all 4.
All inputs are finite; a program needn't handle non-finite values.
Results may differ from the reference program's by a relative error of at most 0.015.
Values may be sent and summed in bfloat16 or wider, within the bound.
No kernel may reach another device: no remote copies, remote signals or barrier semaphores. Data moves between devices by JAX's collectives and lax.ppermute only.
A program may use at most 32 MiB of HBM per device.

```python
import jax
import jax.numpy as jnp
from jax import lax

DM = 3072
HEADS = 16
HD = 128
TILE = 384
NB = 4
TILES_DEV = 2
NTILES = 96
TOKENS = 36864
N_HEAD = 16


def draw_neighbours(key, part):
    tile_ids = jnp.arange(NTILES)
    home = tile_ids // TILES_DEV
    places = jnp.arange(3 * TILES_DEV)
    window = (home[:, None] * TILES_DEV - TILES_DEV + places[None, :]) % NTILES
    own_slot = TILES_DEV + tile_ids % TILES_DEV
    ranks = jax.random.randint(key, (NTILES, 3 * TILES_DEV), 0, 1 << 20) * (3 * TILES_DEV) + places[None, :]
    ranks = jnp.where(places[None, :] == own_slot[:, None], -3, ranks)
    ranks = jnp.where(places[None, :] == own_slot[:, None] - 1, -2, ranks)
    ranks = jnp.where(places[None, :] == own_slot[:, None] + 1, -1, ranks)
    order = jnp.argsort(ranks, axis=1)
    return jnp.take_along_axis(window, order[:, :NB], axis=1).astype(jnp.int32)


def draw_counts(key, part):
    drawn = jax.random.randint(key, (NTILES,), 3, NB + 1)
    return drawn.at[0].set(NB).astype(jnp.int32)


def draw_query_rows(key, part):
    shape = (TOKENS, HEADS * HD)
    noise = 0.4 * jax.random.normal(jax.random.fold_in(key, 1), shape, jnp.float32)
    return noise.astype(jnp.bfloat16)


def draw_key_rows(key, part):
    shape = (TOKENS, HEADS * HD)
    noise = 0.4 * jax.random.normal(jax.random.fold_in(key, 2), shape, jnp.float32)
    return noise.astype(jnp.bfloat16)


def shard_levels(own_key, dims, shards, least, high):
    level = 1.0
    for dim, parts in shards:
        draws = jax.random.uniform(jax.random.fold_in(jax.random.fold_in(own_key, 6), dim), (parts,), jnp.float32, least / len(shards), high / len(shards))
        level = level * jnp.repeat(jnp.exp(draws), dims[dim] // parts).reshape((-1,) + (1,) * (len(dims) - 1 - dim))
    return level


def centred(rng, shape, width, limit, cuts=(), dtype=jnp.bfloat16):
    values = width * jax.random.normal(rng, shape, jnp.float32)
    if cuts:
        values = values * shard_levels(rng, shape, cuts, -0.22, 0.18)
    return jnp.clip(values, -limit, limit).astype(dtype)


def setup_inputs(seed: int = 0) -> dict:
    streams_of = jax.random.split(jax.random.key(seed), 9)
    return {
        "query_rows": draw_query_rows(jax.random.fold_in(streams_of[8], 71), 0),
        "key_rows": draw_key_rows(jax.random.fold_in(streams_of[8], 71), 0),
        "value_rows": centred(streams_of[2], (TOKENS, HEADS * HD), 1.0, 6.0, ((0, 48), (1, 16))),
        "output_rows": centred(streams_of[3], (TOKENS, HEADS * HD), 1.0, 6.0, ((0, 48), (1, 16))),
        "output_grad": centred(streams_of[4], (TOKENS, HEADS * HD), 1.0, 6.0, ((0, 48), (1, 16))),
        "projection": centred(streams_of[5], (3, HEADS * HD, DM), (3 * HEADS * HD) ** -0.5, 0.078125, ((1, 16),)),
        "neighbours": draw_neighbours(jax.random.fold_in(streams_of[8], 71), 0),
        "counts": draw_counts(jax.random.fold_in(streams_of[8], 71), 0),
    }


def reference(query_rows, key_rows, value_rows, output_rows, output_grad, projection, neighbours, counts):
    score_scale = HD ** -0.5
    group_size = HEADS // N_HEAD

    def per_head(carry, head_at):
        total, group_acc = carry
        offset = (head_at * HD).astype(jnp.int32)

        def select(array):
            return lax.dynamic_slice_in_dim(array, offset, HD, 1).reshape(NTILES, TILE, HD)

        queries = select(query_rows)
        keys_all = select(key_rows)
        values_all = select(value_rows)
        outputs = select(output_rows)
        grads_out = select(output_grad)
        deltas = jnp.sum(grads_out.astype(jnp.float32) * outputs.astype(jnp.float32), axis=-1)

        def per_tile(partials, tile_at):
            key_acc, value_acc = partials
            listed = neighbours[tile_at]
            is_live = jnp.arange(NB) < counts[tile_at]
            live_mask = is_live[None, :, None]
            near_keys = keys_all[listed].astype(jnp.float32)
            near_values = values_all[listed].astype(jnp.float32)
            query_tile = queries[tile_at].astype(jnp.float32)
            grad_tile = grads_out[tile_at].astype(jnp.float32)
            scores = jnp.einsum("id,jcd->ijc", query_tile, near_keys) * score_scale
            scores = jnp.where(live_mask, scores, -jnp.inf)
            row_peak = jnp.max(scores, axis=(1, 2))
            raised = jnp.where(live_mask, jnp.exp(scores - row_peak[:, None, None]), 0.0)
            row_total = jnp.sum(raised, axis=(1, 2))
            softmax_weights = (raised / row_total[:, None, None]).astype(jnp.bfloat16)
            prob_grad = jnp.einsum("id,jcd->ijc", grad_tile, near_values)
            score_grad = (softmax_weights.astype(jnp.float32) * (prob_grad - deltas[tile_at][:, None, None]) * score_scale).astype(jnp.bfloat16)
            query_grad = jnp.einsum("ijc,jcd->id", score_grad.astype(jnp.float32), near_keys).astype(jnp.bfloat16)
            key_part = jnp.einsum("ijc,id->jcd", score_grad.astype(jnp.float32), query_tile)
            value_part = jnp.einsum("ijc,id->jcd", softmax_weights.astype(jnp.float32), grad_tile)
            return (key_acc.at[listed].add(key_part), value_acc.at[listed].add(value_part)), query_grad

        zero_tiles = jnp.zeros((NTILES, TILE, HD), jnp.float32)
        (key_acc, value_acc), query_grad = lax.scan(per_tile, (zero_tiles, zero_tiles), jnp.arange(NTILES))
        stacked = jnp.stack([query_grad.reshape(TOKENS, HD), key_acc.astype(jnp.bfloat16).reshape(TOKENS, HD), value_acc.astype(jnp.bfloat16).reshape(TOKENS, HD)])
        weight = lax.dynamic_slice_in_dim(projection, offset, HD, 1)
        group_acc = group_acc + jnp.einsum("cik,ckm->im", stacked.astype(jnp.float32), weight.astype(jnp.float32))
        is_end = (head_at + 1) % group_size == 0
        rounded = lax.optimization_barrier(group_acc.astype(jnp.bfloat16)).astype(jnp.float32)
        total = total + jnp.where(is_end, rounded, jnp.float32(0.0))
        group_acc = jnp.where(is_end, jnp.float32(0.0), group_acc)
        return (total, group_acc), None

    zero_rows = jnp.zeros((TOKENS, DM), jnp.float32)
    (total, _), _ = lax.scan(per_head, (zero_rows, zero_rows), jnp.arange(HEADS))
    return total.astype(jnp.bfloat16)
```

```python
import jax
import jax.numpy as jnp
from jax import lax
from jax.sharding import Mesh
from jax.sharding import PartitionSpec as P

HD = 128
TILE = 384
NB = 4
HEAD_AXES = ("zh", "x", "c")


def with_halo(cells, axis, width):
    count = lax.axis_size(axis)
    head = lax.slice_in_dim(cells, 0, width, axis=1)
    tail = lax.slice_in_dim(cells, cells.shape[1] - width, cells.shape[1], axis=1)
    return jnp.concatenate(
        [
            lax.ppermute(tail, axis, [(i, (i + 1) % count) for i in range(count)]),
            cells,
            lax.ppermute(head, axis, [((i + 1) % count, i) for i in range(count)]),
        ],
        axis=1,
    )


def passed_along(block, axis, distance):
    devices = range(lax.axis_size(axis))
    route = [((i - distance) % len(devices), i) for i in devices]
    return lax.ppermute(block, axis, route)


def pick(array, axis, index):
    return lax.dynamic_index_in_dim(array, index, axis, keepdims=False)


def reduce_scatter(parts):
    c = lax.axis_index("c")
    x = lax.axis_index("x")
    zh = lax.axis_index("zh")
    n_c, n_x, n_zh = parts.shape[3], parts.shape[2], parts.shape[1]
    if n_c > 1:
        got = lax.ppermute(
            pick(parts, 3, 1 - c).astype(jnp.bfloat16), "c", [(0, 1), (1, 0)]
        )
        sums = pick(parts, 3, c) + got.astype(jnp.float32)
    else:
        sums = parts[:, :, :, 0]
    if n_x > 1:
        halves = [sums[:, z] for z in range(n_zh)]
        out = []
        for z, half in enumerate(halves):
            step = 1 if z % 2 == 0 else -1
            route = [(i, (i + step) % n_x) for i in range(n_x)]
            acc = pick(half, 1, (x - step) % n_x)
            for k in range(1, n_x):
                got = lax.ppermute(acc.astype(jnp.bfloat16), "x", route)
                acc = got.astype(jnp.float32) + pick(half, 1, (x - step * (1 + k)) % n_x)
            out.append(acc)
        sums = jnp.stack(out, axis=1)
    else:
        sums = sums[:, :, 0]
    if n_zh > 1:
        route = [(i, (i + 1) % n_zh) for i in range(n_zh)]
        acc = pick(sums, 1, (zh - 1) % n_zh)
        for k in range(1, n_zh):
            got = lax.ppermute(acc.astype(jnp.bfloat16), "zh", route)
            acc = got.astype(jnp.float32) + pick(sums, 1, (zh - 1 - k) % n_zh)
        return acc
    return sums[:, 0]


def local(
    query_rows, key_rows, value_rows, output_rows, output_grad, projection, neighbours, counts
):
    seq_count = lax.axis_size("seq")
    place = lax.axis_index("seq")
    rows_dev = query_rows.shape[0]
    tiles_dev = rows_dev // TILE
    tiles_all = tiles_dev * seq_count
    heads_dev = query_rows.shape[1] // HD
    win = 3 * tiles_dev
    score_scale = HD ** (-0.5)
    first_tile = (place - 1) * tiles_dev
    window = with_halo(jnp.stack([key_rows, value_rows]), "seq", rows_dev)
    key_window = window[0].reshape(win * TILE, heads_dev, HD)
    value_window = window[1].reshape(win * TILE, heads_dev, HD)
    queries = query_rows.reshape(tiles_dev, TILE, heads_dev, HD)
    grads_out = output_grad.reshape(tiles_dev, TILE, heads_dev, HD)
    outputs = output_rows.reshape(tiles_dev, TILE, heads_dev, HD)
    deltas = jnp.sum(grads_out.astype(jnp.float32) * outputs.astype(jnp.float32), axis=-1)
    slot_range = jnp.arange(NB)
    window_ids = jnp.arange(win)
    query_grads = []
    key_acc = jnp.zeros((win * TILE, heads_dev, HD), jnp.float32)
    value_acc = jnp.zeros((win * TILE, heads_dev, HD), jnp.float32)
    for tile_at in range(tiles_dev):
        global_tile = place * tiles_dev + tile_at
        listed = neighbours[global_tile]
        is_live = slot_range < counts[global_tile]
        slots = (listed - first_tile) % tiles_all
        used = jnp.any((slots[:, None] == window_ids[None, :]) & is_live[:, None], axis=0)
        live_mask = jnp.repeat(used, TILE)[None, None, :]
        scores = (
            jnp.einsum(
                "ihd,jhd->hij", queries[tile_at], key_window, preferred_element_type=jnp.float32
            )
            * score_scale
        )
        scores = jnp.where(live_mask, scores, -jnp.inf)
        row_peak = jnp.max(scores, axis=2)
        raised = jnp.where(live_mask, jnp.exp(scores - row_peak[:, :, None]), 0.0)
        row_total = jnp.sum(raised, axis=2)
        softmax_weights = (raised / row_total[:, :, None]).astype(jnp.bfloat16)
        prob_grad = jnp.einsum(
            "ihd,jhd->hij", grads_out[tile_at], value_window, preferred_element_type=jnp.float32
        )
        delta_tile = jnp.transpose(deltas[tile_at], (1, 0))
        score_grad = (
            softmax_weights.astype(jnp.float32)
            * (prob_grad - delta_tile[:, :, None])
            * score_scale
        ).astype(jnp.bfloat16)
        query_grads.append(
            jnp.einsum(
                "hij,jhd->ihd", score_grad, key_window, preferred_element_type=jnp.float32
            ).astype(jnp.bfloat16)
        )
        key_acc = key_acc + jnp.einsum(
            "hij,ihd->jhd", score_grad, queries[tile_at], preferred_element_type=jnp.float32
        )
        value_acc = value_acc + jnp.einsum(
            "hij,ihd->jhd", softmax_weights, grads_out[tile_at], preferred_element_type=jnp.float32
        )
    partials = jnp.stack([key_acc, value_acc])
    from_next = passed_along(partials[:, :rows_dev].astype(jnp.bfloat16), "seq", -1).astype(
        jnp.float32
    )
    from_prev = passed_along(
        partials[:, 2 * rows_dev :].astype(jnp.bfloat16), "seq", 1
    ).astype(jnp.float32)
    owned = partials[:, rows_dev : 2 * rows_dev] + from_next + from_prev
    key_grads = owned[0].astype(jnp.bfloat16).reshape(rows_dev, heads_dev * HD)
    value_grads = owned[1].astype(jnp.bfloat16).reshape(rows_dev, heads_dev * HD)
    grad_stack = jnp.stack(
        [jnp.stack(query_grads).reshape(rows_dev, heads_dev * HD), key_grads, value_grads]
    )
    n_zh, n_x, n_c = (lax.axis_size(a) for a in HEAD_AXES)
    width = projection.shape[2] // (n_zh * n_x * n_c)
    weight = projection.reshape(3, heads_dev * HD, n_zh, n_x, n_c, width)
    parts = jnp.einsum(
        "cik,ckzxym->izxym", grad_stack, weight, preferred_element_type=jnp.float32
    )
    return reduce_scatter(parts).astype(jnp.bfloat16)


def head_shape(n_head):
    n_c = 2 if n_head % 2 == 0 else 1
    n_x = 4 if (n_head // n_c) % 4 == 0 else n_head // n_c
    return n_head // (n_c * n_x), n_x, n_c


def solution(mesh):
    n_seq, n_head = mesh.devices.shape
    split = Mesh(mesh.devices.reshape((n_seq,) + head_shape(n_head)), ("seq",) + HEAD_AXES)
    rows = P("seq", HEAD_AXES)
    in_specs = (rows, rows, rows, rows, rows, P(None, HEAD_AXES, None), P(), P())
    return jax.shard_map(local, mesh=split, in_specs=in_specs, out_specs=rows, check_vma=False)
```

```python
import jax
import jax.numpy as jnp
from jax import lax
from jax.experimental import pallas as pl
from jax.experimental.pallas import tpu as pltpu
from jax.sharding import Mesh
from jax.sharding import PartitionSpec as P

HD = 128
TILE = 384
NB = 4
HEAD_AXES = ("zh", "x", "c")


def with_halo(cells, axis, width):
    count = lax.axis_size(axis)
    head = lax.slice_in_dim(cells, 0, width, axis=1)
    tail = lax.slice_in_dim(cells, cells.shape[1] - width, cells.shape[1], axis=1)
    return jnp.concatenate(
        [
            lax.ppermute(tail, axis, [(i, (i + 1) % count) for i in range(count)]),
            cells,
            lax.ppermute(head, axis, [((i + 1) % count, i) for i in range(count)]),
        ],
        axis=1,
    )


def passed_along(block, axis, distance):
    devices = range(lax.axis_size(axis))
    route = [((i - distance) % len(devices), i) for i in devices]
    return lax.ppermute(block, axis, route)


def pick(array, axis, index):
    return lax.dynamic_index_in_dim(array, index, axis, keepdims=False)


def ring_scatter(block, route_sign, n_x):
    x = lax.axis_index("x")
    rows = block.shape[0]
    halves = [block[: rows // 2], block[rows // 2 :]]
    out = []
    for h, half in enumerate(halves):
        step = route_sign if h == 0 else -route_sign
        route = [(i, (i + step) % n_x) for i in range(n_x)]
        acc = pick(half, 1, (x - step) % n_x)
        for k in range(1, n_x):
            got = lax.ppermute(acc.astype(jnp.bfloat16), "x", route)
            acc = got.astype(jnp.float32) + pick(half, 1, (x - step * (1 + k)) % n_x)
        out.append(acc)
    return jnp.concatenate(out, axis=0)


def reduce_scatter(parts):
    c = lax.axis_index("c")
    zh = lax.axis_index("zh")
    n_c, n_x, n_zh = parts.shape[3], parts.shape[2], parts.shape[1]
    if n_c > 1:
        got = lax.ppermute(
            pick(parts, 3, 1 - c).astype(jnp.bfloat16), "c", [(0, 1), (1, 0)]
        )
        sums = pick(parts, 3, c) + got.astype(jnp.float32)
    else:
        sums = parts[:, :, :, 0]
    if n_zh == 2 and n_x > 1:
        sent = ring_scatter(pick(sums, 1, 1 - zh), 1, n_x).astype(jnp.bfloat16)
        sent, later = lax.optimization_barrier((sent, pick(sums, 1, zh)))
        got = lax.ppermute(sent, "zh", [(0, 1), (1, 0)])
        kept = ring_scatter(later, -1, n_x)
        return kept + got.astype(jnp.float32)
    if n_x > 1:
        sums = jnp.stack([ring_scatter(sums[:, z], 1, n_x) for z in range(n_zh)], axis=1)
    else:
        sums = sums[:, :, 0]
    if n_zh > 1:
        route = [(i, (i + 1) % n_zh) for i in range(n_zh)]
        acc = pick(sums, 1, (zh - 1) % n_zh)
        for k in range(1, n_zh):
            got = lax.ppermute(acc.astype(jnp.bfloat16), "zh", route)
            acc = got.astype(jnp.float32) + pick(sums, 1, (zh - 1 - k) % n_zh)
        return acc
    return sums[:, 0]


def attention_kernel(q_ref, do_ref, o_ref, k_ref, v_ref, mask_ref, dq_ref, dk_ref, dv_ref):
    tile_at = pl.program_id(0)
    score_scale = HD ** (-0.5)
    queries = q_ref[...]
    grads = do_ref[...]
    keys = k_ref[...]
    values = v_ref[...]
    live = mask_ref[0] > 0.0
    contract_last = (((1,), (1,)), ((), ()))
    contract_first = (((0,), (0,)), ((), ()))
    scores = lax.dot_general(queries, keys, contract_last, preferred_element_type=jnp.float32)
    scores = jnp.where(live, scores * score_scale, -jnp.inf)
    row_peak = jnp.max(scores, axis=1, keepdims=True)
    raised = jnp.where(live, jnp.exp(scores - row_peak), 0.0)
    row_total = jnp.sum(raised, axis=1, keepdims=True)
    weights = (raised / row_total).astype(jnp.bfloat16)
    delta = jnp.sum(
        grads.astype(jnp.float32) * o_ref[...].astype(jnp.float32), axis=1, keepdims=True
    )
    prob_grad = lax.dot_general(grads, values, contract_last, preferred_element_type=jnp.float32)
    score_grad = (weights.astype(jnp.float32) * (prob_grad - delta) * score_scale).astype(
        jnp.bfloat16
    )
    dq_ref[...] = jnp.dot(score_grad, keys, preferred_element_type=jnp.float32).astype(
        dq_ref.dtype
    )
    key_part = lax.dot_general(score_grad, queries, contract_first, preferred_element_type=jnp.float32)
    value_part = lax.dot_general(weights, grads, contract_first, preferred_element_type=jnp.float32)

    @pl.when(tile_at == 0)
    def _():
        dk_ref[...] = key_part
        dv_ref[...] = value_part

    @pl.when(tile_at > 0)
    def _():
        dk_ref[...] += key_part
        dv_ref[...] += value_part


def attention(queries, grads, outputs, keys, values, mask):
    rows = queries.shape[0]
    keys_n = keys.shape[0]
    tiles = rows // TILE
    row_spec = pl.BlockSpec((TILE, HD), lambda t: (t, 0))
    whole = pl.BlockSpec((keys_n, HD), lambda t: (0, 0))
    flops = 10 * rows * keys_n * HD
    return pl.pallas_call(
        attention_kernel,
        grid=(tiles,),
        in_specs=[
            row_spec,
            row_spec,
            row_spec,
            whole,
            whole,
            pl.BlockSpec((1, 1, keys_n), lambda t: (t, 0, 0)),
        ],
        out_specs=[row_spec, whole, whole],
        out_shape=[
            jax.ShapeDtypeStruct((rows, HD), jnp.bfloat16),
            jax.ShapeDtypeStruct((keys_n, HD), jnp.float32),
            jax.ShapeDtypeStruct((keys_n, HD), jnp.float32),
        ],
        compiler_params=pltpu.CompilerParams(
            dimension_semantics=("arbitrary",), vmem_limit_bytes=48 * 1024 * 1024
        ),
        cost_estimate=pl.CostEstimate(
            flops=flops,
            transcendentals=rows * keys_n,
            bytes_accessed=2 * (3 * rows * HD + 2 * keys_n * HD) + 8 * keys_n * HD,
        ),
    )(queries, grads, outputs, keys, values, mask)


def local(
    query_rows, key_rows, value_rows, output_rows, output_grad, projection, neighbours, counts
):
    seq_count = lax.axis_size("seq")
    place = lax.axis_index("seq")
    rows_dev = query_rows.shape[0]
    tiles_dev = rows_dev // TILE
    tiles_all = tiles_dev * seq_count
    heads_dev = query_rows.shape[1] // HD
    win = 3 * tiles_dev
    score_scale = HD ** (-0.5)
    first_tile = (place - 1) * tiles_dev
    window = with_halo(jnp.stack([key_rows, value_rows]), "seq", rows_dev)
    key_window = window[0].reshape(win * TILE, heads_dev, HD)
    value_window = window[1].reshape(win * TILE, heads_dev, HD)
    slot_range = jnp.arange(NB)
    window_ids = jnp.arange(win)
    masks = []
    for tile_at in range(tiles_dev):
        global_tile = place * tiles_dev + tile_at
        listed = neighbours[global_tile]
        is_live = slot_range < counts[global_tile]
        slots = (listed - first_tile) % tiles_all
        used = jnp.any((slots[:, None] == window_ids[None, :]) & is_live[:, None], axis=0)
        masks.append(jnp.repeat(used, TILE).astype(jnp.float32))
    mask = jnp.stack(masks)[:, None, :]
    query_grads, key_accs, value_accs = [], [], []
    for head_at in range(heads_dev):
        cols = slice(head_at * HD, (head_at + 1) * HD)
        dq, dk, dv = attention(
            query_rows[:, cols],
            output_grad[:, cols],
            output_rows[:, cols],
            key_window[:, head_at],
            value_window[:, head_at],
            mask,
        )
        query_grads.append(dq)
        key_accs.append(dk)
        value_accs.append(dv)
    key_acc = jnp.stack(key_accs, axis=1)
    value_acc = jnp.stack(value_accs, axis=1)
    partials = jnp.stack([key_acc, value_acc])
    from_next = passed_along(partials[:, :rows_dev].astype(jnp.bfloat16), "seq", -1).astype(
        jnp.float32
    )
    from_prev = passed_along(
        partials[:, 2 * rows_dev :].astype(jnp.bfloat16), "seq", 1
    ).astype(jnp.float32)
    owned = partials[:, rows_dev : 2 * rows_dev] + from_next + from_prev
    key_grads = owned[0].astype(jnp.bfloat16).reshape(rows_dev, heads_dev * HD)
    value_grads = owned[1].astype(jnp.bfloat16).reshape(rows_dev, heads_dev * HD)
    grad_stack = jnp.stack(
        [jnp.concatenate(query_grads, axis=1), key_grads, value_grads]
    )
    n_zh, n_x, n_c = (lax.axis_size(a) for a in HEAD_AXES)
    width = projection.shape[2] // (n_zh * n_x * n_c)
    weight = projection.reshape(3, heads_dev * HD, n_zh, n_x, n_c, width)
    parts = jnp.einsum(
        "cik,ckzxym->izxym", grad_stack, weight, preferred_element_type=jnp.float32
    )
    return reduce_scatter(parts).astype(jnp.bfloat16)


def head_shape(n_head):
    n_c = 2 if n_head % 2 == 0 else 1
    n_x = 4 if (n_head // n_c) % 4 == 0 else n_head // n_c
    return n_head // (n_c * n_x), n_x, n_c


def solution(mesh):
    n_seq, n_head = mesh.devices.shape
    split = Mesh(mesh.devices.reshape((n_seq,) + head_shape(n_head)), ("seq",) + HEAD_AXES)
    rows = P("seq", HEAD_AXES)
    in_specs = (rows, rows, rows, rows, rows, P(None, HEAD_AXES, None), P(), P())
    return jax.shard_map(local, mesh=split, in_specs=in_specs, out_specs=rows, check_vma=False)
```

```python
import jax
import jax.numpy as jnp
from jax import lax
from jax.experimental import pallas as pl
from jax.experimental.pallas import tpu as pltpu
from jax.sharding import Mesh
from jax.sharding import PartitionSpec as P

HD = 128
TILE = 384
NB = 4
HEAD_AXES = ("zh", "x", "c")


def with_halo(cells, axis, width):
    count = lax.axis_size(axis)
    head = lax.slice_in_dim(cells, 0, width, axis=1)
    tail = lax.slice_in_dim(cells, cells.shape[1] - width, cells.shape[1], axis=1)
    return jnp.concatenate(
        [
            lax.ppermute(tail, axis, [(i, (i + 1) % count) for i in range(count)]),
            cells,
            lax.ppermute(head, axis, [((i + 1) % count, i) for i in range(count)]),
        ],
        axis=1,
    )


def passed_along(block, axis, distance):
    devices = range(lax.axis_size(axis))
    route = [((i - distance) % len(devices), i) for i in devices]
    return lax.ppermute(block, axis, route)


def pick(array, axis, index):
    return lax.dynamic_index_in_dim(array, index, axis, keepdims=False)


def ring_scatter(block, route_sign, n_x):
    x = lax.axis_index("x")
    rows = block.shape[0]
    halves = [block[: rows // 2], block[rows // 2 :]]
    out = []
    for h, half in enumerate(halves):
        step = route_sign if h == 0 else -route_sign
        route = [(i, (i + step) % n_x) for i in range(n_x)]
        acc = pick(half, 1, (x - step) % n_x)
        for k in range(1, n_x):
            got = lax.ppermute(acc.astype(jnp.bfloat16), "x", route)
            acc = got.astype(jnp.float32) + pick(half, 1, (x - step * (1 + k)) % n_x)
        out.append(acc)
    return jnp.concatenate(out, axis=0)


def four_scatter(block):
    x = lax.axis_index("x")
    rows = block.shape[0]
    top = slice(0, rows // 2)
    bottom = slice(rows // 2, rows)
    cw = [(i, (i + 1) % 4) for i in range(4)]
    ccw = [(i, (i - 1) % 4) for i in range(4)]
    opposite = pick(block, 1, (x + 2) % 4)
    from_left = lax.ppermute(opposite[top].astype(jnp.bfloat16), "x", cw)
    from_right = lax.ppermute(opposite[bottom].astype(jnp.bfloat16), "x", ccw)
    right = pick(block, 1, (x + 1) % 4)
    left = pick(block, 1, (x - 1) % 4)
    to_right = jnp.concatenate([right[top] + from_left.astype(jnp.float32), right[bottom]])
    to_left = jnp.concatenate([left[top], left[bottom] + from_right.astype(jnp.float32)])
    got_left = lax.ppermute(to_right.astype(jnp.bfloat16), "x", cw)
    got_right = lax.ppermute(to_left.astype(jnp.bfloat16), "x", ccw)
    return pick(block, 1, x) + got_left.astype(jnp.float32) + got_right.astype(jnp.float32)


def reduce_scatter(parts):
    c = lax.axis_index("c")
    zh = lax.axis_index("zh")
    n_c, n_x, n_zh = parts.shape[3], parts.shape[2], parts.shape[1]
    if n_c > 1:
        got = lax.ppermute(
            pick(parts, 3, 1 - c).astype(jnp.bfloat16), "c", [(0, 1), (1, 0)]
        )
        sums = pick(parts, 3, c) + got.astype(jnp.float32)
    else:
        sums = parts[:, :, :, 0]
    if n_x == 4:
        sums = four_scatter(jnp.swapaxes(sums, 1, 2))
    elif n_x > 1:
        sums = jnp.stack([ring_scatter(sums[:, z], 1, n_x) for z in range(n_zh)], axis=1)
    else:
        sums = sums[:, :, 0]
    if n_zh > 1:
        route = [(i, (i + 1) % n_zh) for i in range(n_zh)]
        acc = pick(sums, 1, (zh - 1) % n_zh)
        for k in range(1, n_zh):
            got = lax.ppermute(acc.astype(jnp.bfloat16), "zh", route)
            acc = got.astype(jnp.float32) + pick(sums, 1, (zh - 1 - k) % n_zh)
        return acc
    return sums[:, 0]


def attention_kernel(q_ref, do_ref, o_ref, k_ref, v_ref, mask_ref, dq_ref, dk_ref, dv_ref):
    tile_at = pl.program_id(0)
    score_scale = HD ** (-0.5)
    queries = q_ref[...]
    grads = do_ref[...]
    keys = k_ref[...]
    values = v_ref[...]
    live = mask_ref[0] > 0.0
    contract_last = (((1,), (1,)), ((), ()))
    contract_first = (((0,), (0,)), ((), ()))
    scores = lax.dot_general(queries, keys, contract_last, preferred_element_type=jnp.float32)
    scores = jnp.where(live, scores * score_scale, -jnp.inf)
    row_peak = jnp.max(scores, axis=1, keepdims=True)
    raised = jnp.where(live, jnp.exp(scores - row_peak), 0.0)
    row_total = jnp.sum(raised, axis=1, keepdims=True)
    weights = (raised / row_total).astype(jnp.bfloat16)
    delta = jnp.sum(
        grads.astype(jnp.float32) * o_ref[...].astype(jnp.float32), axis=1, keepdims=True
    )
    prob_grad = lax.dot_general(grads, values, contract_last, preferred_element_type=jnp.float32)
    score_grad = (weights.astype(jnp.float32) * (prob_grad - delta) * score_scale).astype(
        jnp.bfloat16
    )
    dq_ref[...] = jnp.dot(score_grad, keys, preferred_element_type=jnp.float32).astype(
        dq_ref.dtype
    )
    key_part = lax.dot_general(score_grad, queries, contract_first, preferred_element_type=jnp.float32)
    value_part = lax.dot_general(weights, grads, contract_first, preferred_element_type=jnp.float32)

    @pl.when(tile_at == 0)
    def _():
        dk_ref[...] = key_part
        dv_ref[...] = value_part

    @pl.when(tile_at > 0)
    def _():
        dk_ref[...] += key_part
        dv_ref[...] += value_part


def attention(queries, grads, outputs, keys, values, mask):
    rows = queries.shape[0]
    keys_n = keys.shape[0]
    tiles = rows // TILE
    row_spec = pl.BlockSpec((TILE, HD), lambda t: (t, 0))
    whole = pl.BlockSpec((keys_n, HD), lambda t: (0, 0))
    flops = 10 * rows * keys_n * HD
    return pl.pallas_call(
        attention_kernel,
        grid=(tiles,),
        in_specs=[
            row_spec,
            row_spec,
            row_spec,
            whole,
            whole,
            pl.BlockSpec((1, 1, keys_n), lambda t: (t, 0, 0)),
        ],
        out_specs=[row_spec, whole, whole],
        out_shape=[
            jax.ShapeDtypeStruct((rows, HD), jnp.bfloat16),
            jax.ShapeDtypeStruct((keys_n, HD), jnp.float32),
            jax.ShapeDtypeStruct((keys_n, HD), jnp.float32),
        ],
        compiler_params=pltpu.CompilerParams(
            dimension_semantics=("arbitrary",), vmem_limit_bytes=48 * 1024 * 1024
        ),
        cost_estimate=pl.CostEstimate(
            flops=flops,
            transcendentals=rows * keys_n,
            bytes_accessed=2 * (3 * rows * HD + 2 * keys_n * HD) + 8 * keys_n * HD,
        ),
    )(queries, grads, outputs, keys, values, mask)


def local(
    query_rows, key_rows, value_rows, output_rows, output_grad, projection, neighbours, counts
):
    seq_count = lax.axis_size("seq")
    place = lax.axis_index("seq")
    rows_dev = query_rows.shape[0]
    tiles_dev = rows_dev // TILE
    tiles_all = tiles_dev * seq_count
    heads_dev = query_rows.shape[1] // HD
    win = 3 * tiles_dev
    score_scale = HD ** (-0.5)
    first_tile = (place - 1) * tiles_dev
    window = with_halo(jnp.stack([key_rows, value_rows]), "seq", rows_dev)
    key_window = window[0].reshape(win * TILE, heads_dev, HD)
    value_window = window[1].reshape(win * TILE, heads_dev, HD)
    slot_range = jnp.arange(NB)
    window_ids = jnp.arange(win)
    masks = []
    for tile_at in range(tiles_dev):
        global_tile = place * tiles_dev + tile_at
        listed = neighbours[global_tile]
        is_live = slot_range < counts[global_tile]
        slots = (listed - first_tile) % tiles_all
        used = jnp.any((slots[:, None] == window_ids[None, :]) & is_live[:, None], axis=0)
        masks.append(jnp.repeat(used, TILE).astype(jnp.float32))
    mask = jnp.stack(masks)[:, None, :]
    query_grads, key_accs, value_accs = [], [], []
    for head_at in range(heads_dev):
        cols = slice(head_at * HD, (head_at + 1) * HD)
        dq, dk, dv = attention(
            query_rows[:, cols],
            output_grad[:, cols],
            output_rows[:, cols],
            key_window[:, head_at],
            value_window[:, head_at],
            mask,
        )
        query_grads.append(dq)
        key_accs.append(dk)
        value_accs.append(dv)
    key_acc = jnp.stack(key_accs, axis=1)
    value_acc = jnp.stack(value_accs, axis=1)
    partials = jnp.stack([key_acc, value_acc])
    from_next = passed_along(partials[:, :rows_dev].astype(jnp.bfloat16), "seq", -1).astype(
        jnp.float32
    )
    from_prev = passed_along(
        partials[:, 2 * rows_dev :].astype(jnp.bfloat16), "seq", 1
    ).astype(jnp.float32)
    owned = partials[:, rows_dev : 2 * rows_dev] + from_next + from_prev
    key_grads = owned[0].astype(jnp.bfloat16).reshape(rows_dev, heads_dev * HD)
    value_grads = owned[1].astype(jnp.bfloat16).reshape(rows_dev, heads_dev * HD)
    grad_stack = jnp.stack(
        [jnp.concatenate(query_grads, axis=1), key_grads, value_grads]
    )
    n_zh, n_x, n_c = (lax.axis_size(a) for a in HEAD_AXES)
    width = projection.shape[2] // (n_zh * n_x * n_c)
    weight = projection.reshape(3, heads_dev * HD, n_zh, n_x, n_c, width)
    parts = jnp.einsum(
        "cik,ckzxym->izxym", grad_stack, weight, preferred_element_type=jnp.float32
    )
    return reduce_scatter(parts).astype(jnp.bfloat16)


def head_shape(n_head):
    n_c = 2 if n_head % 2 == 0 else 1
    n_x = 4 if (n_head // n_c) % 4 == 0 else n_head // n_c
    return n_head // (n_c * n_x), n_x, n_c


def solution(mesh):
    n_seq, n_head = mesh.devices.shape
    split = Mesh(mesh.devices.reshape((n_seq,) + head_shape(n_head)), ("seq",) + HEAD_AXES)
    rows = P("seq", HEAD_AXES)
    in_specs = (rows, rows, rows, rows, rows, P(None, HEAD_AXES, None), P(), P())
    return jax.shard_map(local, mesh=split, in_specs=in_specs, out_specs=rows, check_vma=False)
```

```python
import jax
import jax.numpy as jnp
from jax import lax
from jax.experimental import pallas as pl
from jax.experimental.pallas import tpu as pltpu
from jax.sharding import Mesh
from jax.sharding import PartitionSpec as P

HD = 128
TILE = 384
NB = 4
HEAD_AXES = ("zh", "x", "c")


def with_halo(cells, axis, width):
    count = lax.axis_size(axis)
    head = lax.slice_in_dim(cells, 0, width, axis=1)
    tail = lax.slice_in_dim(cells, cells.shape[1] - width, cells.shape[1], axis=1)
    return jnp.concatenate(
        [
            lax.ppermute(tail, axis, [(i, (i + 1) % count) for i in range(count)]),
            cells,
            lax.ppermute(head, axis, [((i + 1) % count, i) for i in range(count)]),
        ],
        axis=1,
    )


def passed_along(block, axis, distance):
    devices = range(lax.axis_size(axis))
    route = [((i - distance) % len(devices), i) for i in devices]
    return lax.ppermute(block, axis, route)


def pick(array, axis, index):
    return lax.dynamic_index_in_dim(array, index, axis, keepdims=False)


def ring_scatter(block, route_sign, n_x):
    x = lax.axis_index("x")
    rows = block.shape[0]
    halves = [block[: rows // 2], block[rows // 2 :]]
    out = []
    for h, half in enumerate(halves):
        step = route_sign if h == 0 else -route_sign
        route = [(i, (i + step) % n_x) for i in range(n_x)]
        acc = pick(half, 1, (x - step) % n_x)
        for k in range(1, n_x):
            got = lax.ppermute(acc.astype(jnp.bfloat16), "x", route)
            acc = got.astype(jnp.float32) + pick(half, 1, (x - step * (1 + k)) % n_x)
        out.append(acc)
    return jnp.concatenate(out, axis=0)


def four_scatter(block):
    x = lax.axis_index("x")
    rows = block.shape[0]
    top = slice(0, rows // 2)
    bottom = slice(rows // 2, rows)
    cw = [(i, (i + 1) % 4) for i in range(4)]
    ccw = [(i, (i - 1) % 4) for i in range(4)]
    opposite = pick(block, 1, (x + 2) % 4)
    from_left = lax.ppermute(opposite[top].astype(jnp.bfloat16), "x", cw)
    from_right = lax.ppermute(opposite[bottom].astype(jnp.bfloat16), "x", ccw)
    right = pick(block, 1, (x + 1) % 4)
    left = pick(block, 1, (x - 1) % 4)
    to_right = jnp.concatenate([right[top] + from_left.astype(jnp.float32), right[bottom]])
    to_left = jnp.concatenate([left[top], left[bottom] + from_right.astype(jnp.float32)])
    got_left = lax.ppermute(to_right.astype(jnp.bfloat16), "x", cw)
    got_right = lax.ppermute(to_left.astype(jnp.bfloat16), "x", ccw)
    return pick(block, 1, x) + got_left.astype(jnp.float32) + got_right.astype(jnp.float32)


def reduce_scatter(mine, other):
    zh = lax.axis_index("zh")
    n_x, n_zh = mine.shape[2], mine.shape[1]
    if other is not None:
        got = lax.ppermute(other.astype(jnp.bfloat16), "c", [(0, 1), (1, 0)])
        sums = mine + got.astype(jnp.float32)
    else:
        sums = mine
    if n_x == 4:
        sums = four_scatter(jnp.swapaxes(sums, 1, 2))
    elif n_x > 1:
        sums = jnp.stack([ring_scatter(sums[:, z], 1, n_x) for z in range(n_zh)], axis=1)
    else:
        sums = sums[:, :, 0]
    if n_zh > 1:
        route = [(i, (i + 1) % n_zh) for i in range(n_zh)]
        acc = pick(sums, 1, (zh - 1) % n_zh)
        for k in range(1, n_zh):
            got = lax.ppermute(acc.astype(jnp.bfloat16), "zh", route)
            acc = got.astype(jnp.float32) + pick(sums, 1, (zh - 1 - k) % n_zh)
        return acc
    return sums[:, 0]


def attention_kernel(q_ref, do_ref, o_ref, k_ref, v_ref, mask_ref, dq_ref, dk_ref, dv_ref):
    tile_at = pl.program_id(0)
    score_scale = HD ** (-0.5)
    queries = q_ref[...]
    grads = do_ref[...]
    keys = k_ref[...]
    values = v_ref[...]
    live = mask_ref[0] > 0.0
    contract_last = (((1,), (1,)), ((), ()))
    contract_first = (((0,), (0,)), ((), ()))
    scores = lax.dot_general(queries, keys, contract_last, preferred_element_type=jnp.float32)
    scores = jnp.where(live, scores * score_scale, -jnp.inf)
    row_peak = jnp.max(scores, axis=1, keepdims=True)
    raised = jnp.where(live, jnp.exp(scores - row_peak), 0.0)
    row_total = jnp.sum(raised, axis=1, keepdims=True)
    weights = (raised / row_total).astype(jnp.bfloat16)
    delta = jnp.sum(
        grads.astype(jnp.float32) * o_ref[...].astype(jnp.float32), axis=1, keepdims=True
    )
    prob_grad = lax.dot_general(grads, values, contract_last, preferred_element_type=jnp.float32)
    score_grad = (weights.astype(jnp.float32) * (prob_grad - delta) * score_scale).astype(
        jnp.bfloat16
    )
    dq_ref[...] = jnp.dot(score_grad, keys, preferred_element_type=jnp.float32).astype(
        dq_ref.dtype
    )
    key_part = lax.dot_general(score_grad, queries, contract_first, preferred_element_type=jnp.float32)
    value_part = lax.dot_general(weights, grads, contract_first, preferred_element_type=jnp.float32)

    @pl.when(tile_at == 0)
    def _():
        dk_ref[...] = key_part
        dv_ref[...] = value_part

    @pl.when(tile_at > 0)
    def _():
        dk_ref[...] += key_part
        dv_ref[...] += value_part


def attention(queries, grads, outputs, keys, values, mask):
    rows = queries.shape[0]
    keys_n = keys.shape[0]
    tiles = rows // TILE
    row_spec = pl.BlockSpec((TILE, HD), lambda t: (t, 0))
    whole = pl.BlockSpec((keys_n, HD), lambda t: (0, 0))
    flops = 10 * rows * keys_n * HD
    return pl.pallas_call(
        attention_kernel,
        grid=(tiles,),
        in_specs=[
            row_spec,
            row_spec,
            row_spec,
            whole,
            whole,
            pl.BlockSpec((1, 1, keys_n), lambda t: (t, 0, 0)),
        ],
        out_specs=[row_spec, whole, whole],
        out_shape=[
            jax.ShapeDtypeStruct((rows, HD), jnp.bfloat16),
            jax.ShapeDtypeStruct((keys_n, HD), jnp.float32),
            jax.ShapeDtypeStruct((keys_n, HD), jnp.float32),
        ],
        compiler_params=pltpu.CompilerParams(
            dimension_semantics=("arbitrary",), vmem_limit_bytes=48 * 1024 * 1024
        ),
        cost_estimate=pl.CostEstimate(
            flops=flops,
            transcendentals=rows * keys_n,
            bytes_accessed=2 * (3 * rows * HD + 2 * keys_n * HD) + 8 * keys_n * HD,
        ),
    )(queries, grads, outputs, keys, values, mask)


def local(
    query_rows, key_rows, value_rows, output_rows, output_grad, projection, neighbours, counts
):
    seq_count = lax.axis_size("seq")
    place = lax.axis_index("seq")
    rows_dev = query_rows.shape[0]
    tiles_dev = rows_dev // TILE
    tiles_all = tiles_dev * seq_count
    heads_dev = query_rows.shape[1] // HD
    win = 3 * tiles_dev
    score_scale = HD ** (-0.5)
    first_tile = (place - 1) * tiles_dev
    window = with_halo(jnp.stack([key_rows, value_rows]), "seq", rows_dev)
    key_window = window[0].reshape(win * TILE, heads_dev, HD)
    value_window = window[1].reshape(win * TILE, heads_dev, HD)
    slot_range = jnp.arange(NB)
    window_ids = jnp.arange(win)
    masks = []
    for tile_at in range(tiles_dev):
        global_tile = place * tiles_dev + tile_at
        listed = neighbours[global_tile]
        is_live = slot_range < counts[global_tile]
        slots = (listed - first_tile) % tiles_all
        used = jnp.any((slots[:, None] == window_ids[None, :]) & is_live[:, None], axis=0)
        masks.append(jnp.repeat(used, TILE).astype(jnp.float32))
    mask = jnp.stack(masks)[:, None, :]
    query_grads, key_accs, value_accs = [], [], []
    for head_at in range(heads_dev):
        cols = slice(head_at * HD, (head_at + 1) * HD)
        dq, dk, dv = attention(
            query_rows[:, cols],
            output_grad[:, cols],
            output_rows[:, cols],
            key_window[:, head_at],
            value_window[:, head_at],
            mask,
        )
        query_grads.append(dq)
        key_accs.append(dk)
        value_accs.append(dv)
    key_acc = jnp.stack(key_accs, axis=1)
    value_acc = jnp.stack(value_accs, axis=1)
    partials = jnp.stack([key_acc, value_acc])
    from_next = passed_along(partials[:, :rows_dev].astype(jnp.bfloat16), "seq", -1).astype(
        jnp.float32
    )
    from_prev = passed_along(
        partials[:, 2 * rows_dev :].astype(jnp.bfloat16), "seq", 1
    ).astype(jnp.float32)
    owned = partials[:, rows_dev : 2 * rows_dev] + from_next + from_prev
    key_grads = owned[0].astype(jnp.bfloat16).reshape(rows_dev, heads_dev * HD)
    value_grads = owned[1].astype(jnp.bfloat16).reshape(rows_dev, heads_dev * HD)
    query_grads = jnp.concatenate(query_grads, axis=1)
    return reduce_scatter(*project(query_grads, key_grads, value_grads, projection)).astype(
        jnp.bfloat16
    )


def project(query_grads, key_grads, value_grads, projection):
    n_zh, n_x, n_c = (lax.axis_size(a) for a in HEAD_AXES)
    c = lax.axis_index("c")
    features = projection.shape[1]
    width = projection.shape[2] // (n_zh * n_x * n_c)
    weight = projection.reshape(3, features, n_zh, n_x, n_c, width)
    grads = (query_grads, key_grads, value_grads)

    def term(columns):
        return sum(
            jnp.einsum("ik,kzxm->izxm", g, columns[j], preferred_element_type=jnp.float32)
            for j, g in enumerate(grads)
        )

    mine = term(pick(weight, 4, c))
    other = term(pick(weight, 4, 1 - c)).astype(jnp.bfloat16) if n_c > 1 else None
    return mine, other


def head_shape(n_head):
    n_c = 2 if n_head % 2 == 0 else 1
    n_x = 4 if (n_head // n_c) % 4 == 0 else n_head // n_c
    return n_head // (n_c * n_x), n_x, n_c


def solution(mesh):
    n_seq, n_head = mesh.devices.shape
    split = Mesh(mesh.devices.reshape((n_seq,) + head_shape(n_head)), ("seq",) + HEAD_AXES)
    rows = P("seq", HEAD_AXES)
    in_specs = (rows, rows, rows, rows, rows, P(None, HEAD_AXES, None), P(), P())
    return jax.shard_map(local, mesh=split, in_specs=in_specs, out_specs=rows, check_vma=False)
```

```python
import jax
import jax.numpy as jnp
from jax import lax
from jax.experimental import pallas as pl
from jax.experimental.pallas import tpu as pltpu
from jax.sharding import Mesh
from jax.sharding import PartitionSpec as P

HD = 128
TILE = 384
NB = 4
HEAD_AXES = ("zh", "x", "c")


def with_halo(cells, axis, width):
    count = lax.axis_size(axis)
    head = lax.slice_in_dim(cells, 0, width, axis=1)
    tail = lax.slice_in_dim(cells, cells.shape[1] - width, cells.shape[1], axis=1)
    return jnp.concatenate(
        [
            lax.ppermute(tail, axis, [(i, (i + 1) % count) for i in range(count)]),
            cells,
            lax.ppermute(head, axis, [((i + 1) % count, i) for i in range(count)]),
        ],
        axis=1,
    )


def passed_along(block, axis, distance):
    devices = range(lax.axis_size(axis))
    route = [((i - distance) % len(devices), i) for i in devices]
    return lax.ppermute(block, axis, route)


def pick(array, axis, index):
    return lax.dynamic_index_in_dim(array, index, axis, keepdims=False)


def ring_scatter(block, route_sign, n_x):
    x = lax.axis_index("x")
    rows = block.shape[0]
    halves = [block[: rows // 2], block[rows // 2 :]]
    out = []
    for h, half in enumerate(halves):
        step = route_sign if h == 0 else -route_sign
        route = [(i, (i + step) % n_x) for i in range(n_x)]
        acc = pick(half, 1, (x - step) % n_x)
        for k in range(1, n_x):
            got = lax.ppermute(acc.astype(jnp.bfloat16), "x", route)
            acc = got.astype(jnp.float32) + pick(half, 1, (x - step * (1 + k)) % n_x)
        out.append(acc)
    return jnp.concatenate(out, axis=0)


def four_scatter(block):
    x = lax.axis_index("x")
    rows = block.shape[0]
    top = slice(0, rows // 2)
    bottom = slice(rows // 2, rows)
    cw = [(i, (i + 1) % 4) for i in range(4)]
    ccw = [(i, (i - 1) % 4) for i in range(4)]
    opposite = pick(block, 1, (x + 2) % 4)
    from_left = lax.ppermute(opposite[top].astype(jnp.bfloat16), "x", cw)
    from_right = lax.ppermute(opposite[bottom].astype(jnp.bfloat16), "x", ccw)
    right = pick(block, 1, (x + 1) % 4)
    left = pick(block, 1, (x - 1) % 4)
    to_right = jnp.concatenate([right[top] + from_left.astype(jnp.float32), right[bottom]])
    to_left = jnp.concatenate([left[top], left[bottom] + from_right.astype(jnp.float32)])
    got_left = lax.ppermute(to_right.astype(jnp.bfloat16), "x", cw)
    got_right = lax.ppermute(to_left.astype(jnp.bfloat16), "x", ccw)
    return pick(block, 1, x) + got_left.astype(jnp.float32) + got_right.astype(jnp.float32)


def reduce_scatter(sums):
    zh = lax.axis_index("zh")
    n_x, n_zh = sums.shape[2], sums.shape[1]
    if n_x == 4:
        sums = four_scatter(jnp.swapaxes(sums, 1, 2))
    elif n_x > 1:
        sums = jnp.stack([ring_scatter(sums[:, z], 1, n_x) for z in range(n_zh)], axis=1)
    else:
        sums = sums[:, :, 0]
    if n_zh > 1:
        route = [(i, (i + 1) % n_zh) for i in range(n_zh)]
        acc = pick(sums, 1, (zh - 1) % n_zh)
        for k in range(1, n_zh):
            got = lax.ppermute(acc.astype(jnp.bfloat16), "zh", route)
            acc = got.astype(jnp.float32) + pick(sums, 1, (zh - 1 - k) % n_zh)
        return acc
    return sums[:, 0]


def attention_kernel(q_ref, do_ref, o_ref, k_ref, v_ref, mask_ref, dq_ref, dk_ref, dv_ref):
    tile_at = pl.program_id(0)
    score_scale = HD ** (-0.5)
    queries = q_ref[...]
    grads = do_ref[...]
    keys = k_ref[...]
    values = v_ref[...]
    live = mask_ref[0] > 0.0
    contract_last = (((1,), (1,)), ((), ()))
    contract_first = (((0,), (0,)), ((), ()))
    scores = lax.dot_general(queries, keys, contract_last, preferred_element_type=jnp.float32)
    scores = jnp.where(live, scores * score_scale, -jnp.inf)
    row_peak = jnp.max(scores, axis=1, keepdims=True)
    raised = jnp.where(live, jnp.exp(scores - row_peak), 0.0)
    row_total = jnp.sum(raised, axis=1, keepdims=True)
    weights = (raised / row_total).astype(jnp.bfloat16)
    delta = jnp.sum(
        grads.astype(jnp.float32) * o_ref[...].astype(jnp.float32), axis=1, keepdims=True
    )
    prob_grad = lax.dot_general(grads, values, contract_last, preferred_element_type=jnp.float32)
    score_grad = (weights.astype(jnp.float32) * (prob_grad - delta) * score_scale).astype(
        jnp.bfloat16
    )
    dq_ref[...] = jnp.dot(score_grad, keys, preferred_element_type=jnp.float32).astype(
        dq_ref.dtype
    )
    key_part = lax.dot_general(score_grad, queries, contract_first, preferred_element_type=jnp.float32)
    value_part = lax.dot_general(weights, grads, contract_first, preferred_element_type=jnp.float32)

    @pl.when(tile_at == 0)
    def _():
        dk_ref[...] = key_part
        dv_ref[...] = value_part

    @pl.when(tile_at > 0)
    def _():
        dk_ref[...] += key_part
        dv_ref[...] += value_part


def attention(queries, grads, outputs, keys, values, mask):
    rows = queries.shape[0]
    keys_n = keys.shape[0]
    tiles = rows // TILE
    row_spec = pl.BlockSpec((TILE, HD), lambda t: (t, 0))
    whole = pl.BlockSpec((keys_n, HD), lambda t: (0, 0))
    flops = 10 * rows * keys_n * HD
    return pl.pallas_call(
        attention_kernel,
        grid=(tiles,),
        in_specs=[
            row_spec,
            row_spec,
            row_spec,
            whole,
            whole,
            pl.BlockSpec((1, 1, keys_n), lambda t: (t, 0, 0)),
        ],
        out_specs=[row_spec, whole, whole],
        out_shape=[
            jax.ShapeDtypeStruct((rows, HD), jnp.bfloat16),
            jax.ShapeDtypeStruct((keys_n, HD), jnp.float32),
            jax.ShapeDtypeStruct((keys_n, HD), jnp.float32),
        ],
        compiler_params=pltpu.CompilerParams(
            dimension_semantics=("arbitrary",), vmem_limit_bytes=48 * 1024 * 1024
        ),
        cost_estimate=pl.CostEstimate(
            flops=flops,
            transcendentals=rows * keys_n,
            bytes_accessed=2 * (3 * rows * HD + 2 * keys_n * HD) + 8 * keys_n * HD,
        ),
    )(queries, grads, outputs, keys, values, mask)


def local(
    query_rows, key_rows, value_rows, output_rows, output_grad, projection, neighbours, counts
):
    seq_count = lax.axis_size("seq")
    place = lax.axis_index("seq")
    rows_dev = query_rows.shape[0]
    tiles_dev = rows_dev // TILE
    tiles_all = tiles_dev * seq_count
    heads_dev = query_rows.shape[1] // HD
    win = 3 * tiles_dev
    score_scale = HD ** (-0.5)
    first_tile = (place - 1) * tiles_dev
    weights = core_weights(projection)
    window = with_halo(jnp.stack([key_rows, value_rows]), "seq", rows_dev)
    key_window = window[0].reshape(win * TILE, heads_dev, HD)
    value_window = window[1].reshape(win * TILE, heads_dev, HD)
    slot_range = jnp.arange(NB)
    window_ids = jnp.arange(win)
    masks = []
    for tile_at in range(tiles_dev):
        global_tile = place * tiles_dev + tile_at
        listed = neighbours[global_tile]
        is_live = slot_range < counts[global_tile]
        slots = (listed - first_tile) % tiles_all
        used = jnp.any((slots[:, None] == window_ids[None, :]) & is_live[:, None], axis=0)
        masks.append(jnp.repeat(used, TILE).astype(jnp.float32))
    mask = jnp.stack(masks)[:, None, :]
    query_grads, key_accs, value_accs = [], [], []
    for head_at in range(heads_dev):
        cols = slice(head_at * HD, (head_at + 1) * HD)
        dq, dk, dv = attention(
            query_rows[:, cols],
            output_grad[:, cols],
            output_rows[:, cols],
            key_window[:, head_at],
            value_window[:, head_at],
            mask,
        )
        query_grads.append(dq)
        key_accs.append(dk)
        value_accs.append(dv)
    query_grads = jnp.concatenate(query_grads, axis=1)
    key_acc = jnp.stack(key_accs, axis=1)
    value_acc = jnp.stack(value_accs, axis=1)
    partials = jnp.stack([key_acc, value_acc])
    from_next = passed_along(partials[:, :rows_dev].astype(jnp.bfloat16), "seq", -1).astype(
        jnp.float32
    )
    from_prev = passed_along(
        partials[:, 2 * rows_dev :].astype(jnp.bfloat16), "seq", 1
    ).astype(jnp.float32)
    owned = partials[:, rows_dev : 2 * rows_dev] + from_next + from_prev
    key_grads = owned[0].astype(jnp.bfloat16).reshape(rows_dev, heads_dev * HD)
    value_grads = owned[1].astype(jnp.bfloat16).reshape(rows_dev, heads_dev * HD)
    sums = project((query_grads, key_grads, value_grads), weights)
    return reduce_scatter(sums).astype(jnp.bfloat16)


def core_weights(projection):
    n_zh, n_x, n_c = (lax.axis_size(a) for a in HEAD_AXES)
    c = lax.axis_index("c")
    features = projection.shape[1]
    width = projection.shape[2] // (n_zh * n_x * n_c)
    weight = projection.reshape(3, features, n_zh, n_x, n_c, width)
    mine = pick(weight, 4, c)
    if n_c == 1:
        return mine, None
    partner = lax.ppermute(pick(weight, 4, 1 - c), "c", [(0, 1), (1, 0)])
    return mine, partner


def project(grads, weights):
    mine_w, partner_w = weights
    total = 0.0
    for j, g in enumerate(grads):
        total = total + jnp.einsum("ik,kzxm->izxm", g, mine_w[j], preferred_element_type=jnp.float32)
        if partner_w is not None:
            got = lax.ppermute(g, "c", [(0, 1), (1, 0)])
            total = total + jnp.einsum(
                "ik,kzxm->izxm", got, partner_w[j], preferred_element_type=jnp.float32
            )
    return total


def head_shape(n_head):
    n_c = 2 if n_head % 2 == 0 else 1
    n_x = 4 if (n_head // n_c) % 4 == 0 else n_head // n_c
    return n_head // (n_c * n_x), n_x, n_c


def solution(mesh):
    n_seq, n_head = mesh.devices.shape
    split = Mesh(mesh.devices.reshape((n_seq,) + head_shape(n_head)), ("seq",) + HEAD_AXES)
    rows = P("seq", HEAD_AXES)
    in_specs = (rows, rows, rows, rows, rows, P(None, HEAD_AXES, None), P(), P())
    return jax.shard_map(local, mesh=split, in_specs=in_specs, out_specs=rows, check_vma=False)
```

```python
import jax
import jax.numpy as jnp
from jax import lax
from jax.experimental import pallas as pl
from jax.experimental.pallas import tpu as pltpu
from jax.sharding import Mesh
from jax.sharding import PartitionSpec as P

HD = 128
TILE = 384
NB = 4
HEAD_AXES = ("zh", "x", "c")


def with_halo(cells, axis, width):
    count = lax.axis_size(axis)
    head = lax.slice_in_dim(cells, 0, width, axis=1)
    tail = lax.slice_in_dim(cells, cells.shape[1] - width, cells.shape[1], axis=1)
    return jnp.concatenate(
        [
            lax.ppermute(tail, axis, [(i, (i + 1) % count) for i in range(count)]),
            cells,
            lax.ppermute(head, axis, [((i + 1) % count, i) for i in range(count)]),
        ],
        axis=1,
    )


def passed_along(block, axis, distance):
    devices = range(lax.axis_size(axis))
    route = [((i - distance) % len(devices), i) for i in devices]
    return lax.ppermute(block, axis, route)


def pick(array, axis, index):
    return lax.dynamic_index_in_dim(array, index, axis, keepdims=False)


def ring_scatter(block, route_sign, n_x):
    x = lax.axis_index("x")
    rows = block.shape[0]
    halves = [block[: rows // 2], block[rows // 2 :]]
    out = []
    for h, half in enumerate(halves):
        step = route_sign if h == 0 else -route_sign
        route = [(i, (i + step) % n_x) for i in range(n_x)]
        acc = pick(half, 1, (x - step) % n_x)
        for k in range(1, n_x):
            got = lax.ppermute(acc.astype(jnp.bfloat16), "x", route)
            acc = got.astype(jnp.float32) + pick(half, 1, (x - step * (1 + k)) % n_x)
        out.append(acc)
    return jnp.concatenate(out, axis=0)


def four_scatter(block):
    x = lax.axis_index("x")
    rows = block.shape[0]
    top = slice(0, rows // 2)
    bottom = slice(rows // 2, rows)
    cw = [(i, (i + 1) % 4) for i in range(4)]
    ccw = [(i, (i - 1) % 4) for i in range(4)]
    opposite = pick(block, 1, (x + 2) % 4)
    from_left = lax.ppermute(opposite[top].astype(jnp.bfloat16), "x", cw)
    from_right = lax.ppermute(opposite[bottom].astype(jnp.bfloat16), "x", ccw)
    right = pick(block, 1, (x + 1) % 4)
    left = pick(block, 1, (x - 1) % 4)
    to_right = jnp.concatenate([right[top] + from_left.astype(jnp.float32), right[bottom]])
    to_left = jnp.concatenate([left[top], left[bottom] + from_right.astype(jnp.float32)])
    got_left = lax.ppermute(to_right.astype(jnp.bfloat16), "x", cw)
    got_right = lax.ppermute(to_left.astype(jnp.bfloat16), "x", ccw)
    return pick(block, 1, x) + got_left.astype(jnp.float32) + got_right.astype(jnp.float32)


def reduce_scatter(parts):
    c = lax.axis_index("c")
    zh = lax.axis_index("zh")
    n_c, n_x, n_zh = parts.shape[3], parts.shape[2], parts.shape[1]
    if n_c > 1:
        got = lax.ppermute(pick(parts, 3, 1 - c), "c", [(0, 1), (1, 0)])
        sums = pick(parts, 3, c).astype(jnp.float32) + got.astype(jnp.float32)
    else:
        sums = parts[:, :, :, 0].astype(jnp.float32)
    if n_x == 4:
        sums = four_scatter(jnp.swapaxes(sums, 1, 2))
    elif n_x > 1:
        sums = jnp.stack([ring_scatter(sums[:, z], 1, n_x) for z in range(n_zh)], axis=1)
    else:
        sums = sums[:, :, 0]
    if n_zh > 1:
        route = [(i, (i + 1) % n_zh) for i in range(n_zh)]
        acc = pick(sums, 1, (zh - 1) % n_zh)
        for k in range(1, n_zh):
            got = lax.ppermute(acc.astype(jnp.bfloat16), "zh", route)
            acc = got.astype(jnp.float32) + pick(sums, 1, (zh - 1 - k) % n_zh)
        return acc
    return sums[:, 0]


def attention_kernel(q_ref, do_ref, o_ref, k_ref, v_ref, mask_ref, dq_ref, dk_ref, dv_ref):
    tile_at = pl.program_id(0)
    score_scale = HD ** (-0.5)
    queries = q_ref[...]
    grads = do_ref[...]
    keys = k_ref[...]
    values = v_ref[...]
    live = mask_ref[0] > 0.0
    contract_last = (((1,), (1,)), ((), ()))
    contract_first = (((0,), (0,)), ((), ()))
    scores = lax.dot_general(queries, keys, contract_last, preferred_element_type=jnp.float32)
    scores = jnp.where(live, scores * score_scale, -jnp.inf)
    row_peak = jnp.max(scores, axis=1, keepdims=True)
    raised = jnp.where(live, jnp.exp(scores - row_peak), 0.0)
    row_total = jnp.sum(raised, axis=1, keepdims=True)
    weights = (raised / row_total).astype(jnp.bfloat16)
    delta = jnp.sum(
        grads.astype(jnp.float32) * o_ref[...].astype(jnp.float32), axis=1, keepdims=True
    )
    prob_grad = lax.dot_general(grads, values, contract_last, preferred_element_type=jnp.float32)
    score_grad = (weights.astype(jnp.float32) * (prob_grad - delta) * score_scale).astype(
        jnp.bfloat16
    )
    dq_ref[...] = jnp.dot(score_grad, keys, preferred_element_type=jnp.float32).astype(
        dq_ref.dtype
    )
    key_part = lax.dot_general(score_grad, queries, contract_first, preferred_element_type=jnp.float32)
    value_part = lax.dot_general(weights, grads, contract_first, preferred_element_type=jnp.float32)

    @pl.when(tile_at == 0)
    def _():
        dk_ref[...] = key_part
        dv_ref[...] = value_part

    @pl.when(tile_at > 0)
    def _():
        dk_ref[...] += key_part
        dv_ref[...] += value_part


def attention(queries, grads, outputs, keys, values, mask):
    rows = queries.shape[0]
    keys_n = keys.shape[0]
    tiles = rows // TILE
    row_spec = pl.BlockSpec((TILE, HD), lambda t: (t, 0))
    whole = pl.BlockSpec((keys_n, HD), lambda t: (0, 0))
    flops = 10 * rows * keys_n * HD
    return pl.pallas_call(
        attention_kernel,
        grid=(tiles,),
        in_specs=[
            row_spec,
            row_spec,
            row_spec,
            whole,
            whole,
            pl.BlockSpec((1, 1, keys_n), lambda t: (t, 0, 0)),
        ],
        out_specs=[row_spec, whole, whole],
        out_shape=[
            jax.ShapeDtypeStruct((rows, HD), jnp.bfloat16),
            jax.ShapeDtypeStruct((keys_n, HD), jnp.float32),
            jax.ShapeDtypeStruct((keys_n, HD), jnp.float32),
        ],
        compiler_params=pltpu.CompilerParams(
            dimension_semantics=("arbitrary",), vmem_limit_bytes=48 * 1024 * 1024
        ),
        cost_estimate=pl.CostEstimate(
            flops=flops,
            transcendentals=rows * keys_n,
            bytes_accessed=2 * (3 * rows * HD + 2 * keys_n * HD) + 8 * keys_n * HD,
        ),
    )(queries, grads, outputs, keys, values, mask)


def local(
    query_rows, key_rows, value_rows, output_rows, output_grad, projection, neighbours, counts
):
    seq_count = lax.axis_size("seq")
    place = lax.axis_index("seq")
    rows_dev = query_rows.shape[0]
    tiles_dev = rows_dev // TILE
    tiles_all = tiles_dev * seq_count
    heads_dev = query_rows.shape[1] // HD
    win = 3 * tiles_dev
    score_scale = HD ** (-0.5)
    first_tile = (place - 1) * tiles_dev
    window = with_halo(jnp.stack([key_rows, value_rows]), "seq", rows_dev)
    key_window = window[0].reshape(win * TILE, heads_dev, HD)
    value_window = window[1].reshape(win * TILE, heads_dev, HD)
    slot_range = jnp.arange(NB)
    window_ids = jnp.arange(win)
    masks = []
    for tile_at in range(tiles_dev):
        global_tile = place * tiles_dev + tile_at
        listed = neighbours[global_tile]
        is_live = slot_range < counts[global_tile]
        slots = (listed - first_tile) % tiles_all
        used = jnp.any((slots[:, None] == window_ids[None, :]) & is_live[:, None], axis=0)
        masks.append(jnp.repeat(used, TILE).astype(jnp.float32))
    mask = jnp.stack(masks)[:, None, :]
    query_grads, key_accs, value_accs = [], [], []
    for head_at in range(heads_dev):
        cols = slice(head_at * HD, (head_at + 1) * HD)
        dq, dk, dv = attention(
            query_rows[:, cols],
            output_grad[:, cols],
            output_rows[:, cols],
            key_window[:, head_at],
            value_window[:, head_at],
            mask,
        )
        query_grads.append(dq)
        key_accs.append(dk)
        value_accs.append(dv)
    key_acc = jnp.stack(key_accs, axis=1)
    value_acc = jnp.stack(value_accs, axis=1)
    partials = jnp.stack([key_acc, value_acc])
    from_next = passed_along(partials[:, :rows_dev].astype(jnp.bfloat16), "seq", -1).astype(
        jnp.float32
    )
    from_prev = passed_along(
        partials[:, 2 * rows_dev :].astype(jnp.bfloat16), "seq", 1
    ).astype(jnp.float32)
    owned = partials[:, rows_dev : 2 * rows_dev] + from_next + from_prev
    key_grads = owned[0].astype(jnp.bfloat16).reshape(rows_dev, heads_dev * HD)
    value_grads = owned[1].astype(jnp.bfloat16).reshape(rows_dev, heads_dev * HD)
    grad_stack = jnp.stack(
        [jnp.concatenate(query_grads, axis=1), key_grads, value_grads]
    )
    n_zh, n_x, n_c = (lax.axis_size(a) for a in HEAD_AXES)
    width = projection.shape[2] // (n_zh * n_x * n_c)
    weight = projection.reshape(3, heads_dev * HD, n_zh, n_x, n_c, width)
    parts = jnp.einsum(
        "cik,ckzxym->izxym", grad_stack, weight, preferred_element_type=jnp.float32
    ).astype(jnp.bfloat16)
    return reduce_scatter(parts).astype(jnp.bfloat16)


def head_shape(n_head):
    n_c = 2 if n_head % 2 == 0 else 1
    n_x = 4 if (n_head // n_c) % 4 == 0 else n_head // n_c
    return n_head // (n_c * n_x), n_x, n_c


def solution(mesh):
    n_seq, n_head = mesh.devices.shape
    split = Mesh(mesh.devices.reshape((n_seq,) + head_shape(n_head)), ("seq",) + HEAD_AXES)
    rows = P("seq", HEAD_AXES)
    in_specs = (rows, rows, rows, rows, rows, P(None, HEAD_AXES, None), P(), P())
    return jax.shard_map(local, mesh=split, in_specs=in_specs, out_specs=rows, check_vma=False)
```

```python
import jax
import jax.numpy as jnp
from jax import lax
from jax.experimental import pallas as pl
from jax.experimental.pallas import tpu as pltpu
from jax.sharding import Mesh
from jax.sharding import PartitionSpec as P

HD = 128
TILE = 384
NB = 4
HEAD_AXES = ("zh", "x", "c")


def with_halo(cells, axis, width):
    count = lax.axis_size(axis)
    head = lax.slice_in_dim(cells, 0, width, axis=1)
    tail = lax.slice_in_dim(cells, cells.shape[1] - width, cells.shape[1], axis=1)
    return jnp.concatenate(
        [
            lax.ppermute(tail, axis, [(i, (i + 1) % count) for i in range(count)]),
            cells,
            lax.ppermute(head, axis, [((i + 1) % count, i) for i in range(count)]),
        ],
        axis=1,
    )


def passed_along(block, axis, distance):
    devices = range(lax.axis_size(axis))
    route = [((i - distance) % len(devices), i) for i in devices]
    return lax.ppermute(block, axis, route)


def pick(array, axis, index):
    return lax.dynamic_index_in_dim(array, index, axis, keepdims=False)


def ring_scatter(block, route_sign, n_x):
    x = lax.axis_index("x")
    rows = block.shape[0]
    halves = [block[: rows // 2], block[rows // 2 :]]
    out = []
    for h, half in enumerate(halves):
        step = route_sign if h == 0 else -route_sign
        route = [(i, (i + step) % n_x) for i in range(n_x)]
        acc = pick(half, 1, (x - step) % n_x)
        for k in range(1, n_x):
            got = lax.ppermute(acc.astype(jnp.bfloat16), "x", route)
            acc = got.astype(jnp.float32) + pick(half, 1, (x - step * (1 + k)) % n_x)
        out.append(acc)
    return jnp.concatenate(out, axis=0)


def four_scatter(block):
    x = lax.axis_index("x")
    rows = block.shape[0]
    top = slice(0, rows // 2)
    bottom = slice(rows // 2, rows)
    cw = [(i, (i + 1) % 4) for i in range(4)]
    ccw = [(i, (i - 1) % 4) for i in range(4)]
    opposite = pick(block, 1, (x + 2) % 4)
    from_left = lax.ppermute(opposite[top].astype(jnp.bfloat16), "x", cw)
    from_right = lax.ppermute(opposite[bottom].astype(jnp.bfloat16), "x", ccw)
    right = pick(block, 1, (x + 1) % 4)
    left = pick(block, 1, (x - 1) % 4)
    to_right = jnp.concatenate([right[top] + from_left.astype(jnp.float32), right[bottom]])
    to_left = jnp.concatenate([left[top], left[bottom] + from_right.astype(jnp.float32)])
    got_left = lax.ppermute(to_right.astype(jnp.bfloat16), "x", cw)
    got_right = lax.ppermute(to_left.astype(jnp.bfloat16), "x", ccw)
    return pick(block, 1, x) + got_left.astype(jnp.float32) + got_right.astype(jnp.float32)


def reduce_scatter(sums):
    zh = lax.axis_index("zh")
    n_x, n_zh = sums.shape[2], sums.shape[1]
    if n_x == 4:
        sums = four_scatter(jnp.swapaxes(sums, 1, 2))
    elif n_x > 1:
        sums = jnp.stack([ring_scatter(sums[:, z], 1, n_x) for z in range(n_zh)], axis=1)
    else:
        sums = sums[:, :, 0]
    if n_zh > 1:
        route = [(i, (i + 1) % n_zh) for i in range(n_zh)]
        acc = pick(sums, 1, (zh - 1) % n_zh)
        for k in range(1, n_zh):
            got = lax.ppermute(acc.astype(jnp.bfloat16), "zh", route)
            acc = got.astype(jnp.float32) + pick(sums, 1, (zh - 1 - k) % n_zh)
        return acc
    return sums[:, 0]


def attention_kernel(q_ref, do_ref, o_ref, k_ref, v_ref, mask_ref, dq_ref, dk_ref, dv_ref):
    tile_at = pl.program_id(0)
    score_scale = HD ** (-0.5)
    queries = q_ref[...]
    grads = do_ref[...]
    keys = k_ref[...]
    values = v_ref[...]
    live = mask_ref[0] > 0.0
    contract_last = (((1,), (1,)), ((), ()))
    contract_first = (((0,), (0,)), ((), ()))
    scores = lax.dot_general(queries, keys, contract_last, preferred_element_type=jnp.float32)
    scores = jnp.where(live, scores * score_scale, -jnp.inf)
    row_peak = jnp.max(scores, axis=1, keepdims=True)
    raised = jnp.where(live, jnp.exp(scores - row_peak), 0.0)
    row_total = jnp.sum(raised, axis=1, keepdims=True)
    weights = (raised / row_total).astype(jnp.bfloat16)
    delta = jnp.sum(
        grads.astype(jnp.float32) * o_ref[...].astype(jnp.float32), axis=1, keepdims=True
    )
    prob_grad = lax.dot_general(grads, values, contract_last, preferred_element_type=jnp.float32)
    score_grad = (weights.astype(jnp.float32) * (prob_grad - delta) * score_scale).astype(
        jnp.bfloat16
    )
    dq_ref[...] = jnp.dot(score_grad, keys, preferred_element_type=jnp.float32).astype(
        dq_ref.dtype
    )
    key_part = lax.dot_general(score_grad, queries, contract_first, preferred_element_type=jnp.float32)
    value_part = lax.dot_general(weights, grads, contract_first, preferred_element_type=jnp.float32)

    @pl.when(tile_at == 0)
    def _():
        dk_ref[...] = key_part
        dv_ref[...] = value_part

    @pl.when(tile_at > 0)
    def _():
        dk_ref[...] += key_part
        dv_ref[...] += value_part


def attention(queries, grads, outputs, keys, values, mask):
    rows = queries.shape[0]
    keys_n = keys.shape[0]
    tiles = rows // TILE
    row_spec = pl.BlockSpec((TILE, HD), lambda t: (t, 0))
    whole = pl.BlockSpec((keys_n, HD), lambda t: (0, 0))
    flops = 10 * rows * keys_n * HD
    return pl.pallas_call(
        attention_kernel,
        grid=(tiles,),
        in_specs=[
            row_spec,
            row_spec,
            row_spec,
            whole,
            whole,
            pl.BlockSpec((1, 1, keys_n), lambda t: (t, 0, 0)),
        ],
        out_specs=[row_spec, whole, whole],
        out_shape=[
            jax.ShapeDtypeStruct((rows, HD), jnp.bfloat16),
            jax.ShapeDtypeStruct((keys_n, HD), jnp.float32),
            jax.ShapeDtypeStruct((keys_n, HD), jnp.float32),
        ],
        compiler_params=pltpu.CompilerParams(
            dimension_semantics=("arbitrary",), vmem_limit_bytes=48 * 1024 * 1024
        ),
        cost_estimate=pl.CostEstimate(
            flops=flops,
            transcendentals=rows * keys_n,
            bytes_accessed=2 * (3 * rows * HD + 2 * keys_n * HD) + 8 * keys_n * HD,
        ),
    )(queries, grads, outputs, keys, values, mask)


def local(
    query_rows, key_rows, value_rows, output_rows, output_grad, projection, neighbours, counts
):
    seq_count = lax.axis_size("seq")
    place = lax.axis_index("seq")
    rows_dev = query_rows.shape[0]
    tiles_dev = rows_dev // TILE
    tiles_all = tiles_dev * seq_count
    heads_dev = query_rows.shape[1] // HD
    win = 3 * tiles_dev
    score_scale = HD ** (-0.5)
    first_tile = (place - 1) * tiles_dev
    window = with_halo(jnp.stack([key_rows, value_rows]), "seq", rows_dev)
    key_window = window[0].reshape(win * TILE, heads_dev, HD)
    value_window = window[1].reshape(win * TILE, heads_dev, HD)
    slot_range = jnp.arange(NB)
    window_ids = jnp.arange(win)
    masks = []
    for tile_at in range(tiles_dev):
        global_tile = place * tiles_dev + tile_at
        listed = neighbours[global_tile]
        is_live = slot_range < counts[global_tile]
        slots = (listed - first_tile) % tiles_all
        used = jnp.any((slots[:, None] == window_ids[None, :]) & is_live[:, None], axis=0)
        masks.append(jnp.repeat(used, TILE).astype(jnp.float32))
    mask = jnp.stack(masks)[:, None, :]
    query_grads, key_accs, value_accs = [], [], []
    for head_at in range(heads_dev):
        cols = slice(head_at * HD, (head_at + 1) * HD)
        dq, dk, dv = attention(
            query_rows[:, cols],
            output_grad[:, cols],
            output_rows[:, cols],
            key_window[:, head_at],
            value_window[:, head_at],
            mask,
        )
        query_grads.append(dq)
        key_accs.append(dk)
        value_accs.append(dv)
    key_acc = jnp.stack(key_accs, axis=1)
    value_acc = jnp.stack(value_accs, axis=1)
    partials = jnp.stack([key_acc, value_acc])
    from_next = passed_along(partials[:, :rows_dev].astype(jnp.bfloat16), "seq", -1).astype(
        jnp.float32
    )
    from_prev = passed_along(
        partials[:, 2 * rows_dev :].astype(jnp.bfloat16), "seq", 1
    ).astype(jnp.float32)
    owned = partials[:, rows_dev : 2 * rows_dev] + from_next + from_prev
    key_grads = owned[0].astype(jnp.bfloat16).reshape(rows_dev, heads_dev * HD)
    value_grads = owned[1].astype(jnp.bfloat16).reshape(rows_dev, heads_dev * HD)
    grad_stack = jnp.stack(
        [jnp.concatenate(query_grads, axis=1), key_grads, value_grads]
    )
    n_zh, n_x, n_c = (lax.axis_size(a) for a in HEAD_AXES)
    width = projection.shape[2] // (n_zh * n_x * n_c)
    weight = projection.reshape(3, heads_dev * HD, n_zh, n_x, n_c, width)
    c = lax.axis_index("c")

    def term(columns):
        return jnp.einsum("cik,ckzxm->izxm", grad_stack, columns, preferred_element_type=jnp.float32)

    if n_c > 1:
        other = term(pick(weight, 4, 1 - c)).astype(jnp.bfloat16)
        got = lax.ppermute(other, "c", [(0, 1), (1, 0)])
        mine = term(pick(weight, 4, c)).astype(jnp.bfloat16)
        sums = mine.astype(jnp.float32) + got.astype(jnp.float32)
    else:
        sums = term(weight[:, :, :, :, 0]).astype(jnp.bfloat16).astype(jnp.float32)
    return reduce_scatter(sums).astype(jnp.bfloat16)


def head_shape(n_head):
    n_c = 2 if n_head % 2 == 0 else 1
    n_x = 4 if (n_head // n_c) % 4 == 0 else n_head // n_c
    return n_head // (n_c * n_x), n_x, n_c


def solution(mesh):
    n_seq, n_head = mesh.devices.shape
    split = Mesh(mesh.devices.reshape((n_seq,) + head_shape(n_head)), ("seq",) + HEAD_AXES)
    rows = P("seq", HEAD_AXES)
    in_specs = (rows, rows, rows, rows, rows, P(None, HEAD_AXES, None), P(), P())
    return jax.shard_map(local, mesh=split, in_specs=in_specs, out_specs=rows, check_vma=False)
```

```python
import jax
import jax.numpy as jnp
from jax import lax
from jax.experimental import pallas as pl
from jax.experimental.pallas import tpu as pltpu
from jax.sharding import Mesh
from jax.sharding import PartitionSpec as P

HD = 128
TILE = 384
NB = 4
HEAD_AXES = ("zh", "x", "c")


def with_halo(cells, axis, width):
    count = lax.axis_size(axis)
    head = lax.slice_in_dim(cells, 0, width, axis=1)
    tail = lax.slice_in_dim(cells, cells.shape[1] - width, cells.shape[1], axis=1)
    return jnp.concatenate(
        [
            lax.ppermute(tail, axis, [(i, (i + 1) % count) for i in range(count)]),
            cells,
            lax.ppermute(head, axis, [((i + 1) % count, i) for i in range(count)]),
        ],
        axis=1,
    )


def passed_along(block, axis, distance):
    devices = range(lax.axis_size(axis))
    route = [((i - distance) % len(devices), i) for i in devices]
    return lax.ppermute(block, axis, route)


def pick(array, axis, index):
    return lax.dynamic_index_in_dim(array, index, axis, keepdims=False)


def ring_scatter(block, route_sign, n_x):
    x = lax.axis_index("x")
    rows = block.shape[0]
    halves = [block[: rows // 2], block[rows // 2 :]]
    out = []
    for h, half in enumerate(halves):
        step = route_sign if h == 0 else -route_sign
        route = [(i, (i + step) % n_x) for i in range(n_x)]
        acc = pick(half, 1, (x - step) % n_x)
        for k in range(1, n_x):
            got = lax.ppermute(acc.astype(jnp.bfloat16), "x", route)
            acc = got.astype(jnp.float32) + pick(half, 1, (x - step * (1 + k)) % n_x)
        out.append(acc)
    return jnp.concatenate(out, axis=0)


def four_scatter(block):
    x = lax.axis_index("x")
    rows = block.shape[0]
    top = slice(0, rows // 2)
    bottom = slice(rows // 2, rows)
    cw = [(i, (i + 1) % 4) for i in range(4)]
    ccw = [(i, (i - 1) % 4) for i in range(4)]
    opposite = pick(block, 1, (x + 2) % 4)
    from_left = lax.ppermute(opposite[top].astype(jnp.bfloat16), "x", cw)
    from_right = lax.ppermute(opposite[bottom].astype(jnp.bfloat16), "x", ccw)
    right = pick(block, 1, (x + 1) % 4)
    left = pick(block, 1, (x - 1) % 4)
    to_right = jnp.concatenate([right[top] + from_left.astype(jnp.float32), right[bottom]])
    to_left = jnp.concatenate([left[top], left[bottom] + from_right.astype(jnp.float32)])
    got_left = lax.ppermute(to_right.astype(jnp.bfloat16), "x", cw)
    got_right = lax.ppermute(to_left.astype(jnp.bfloat16), "x", ccw)
    return pick(block, 1, x) + got_left.astype(jnp.float32) + got_right.astype(jnp.float32)


def four_then_pair(block):
    x = lax.axis_index("x")
    zh = lax.axis_index("zh")
    rows = block.shape[0]
    top = slice(0, rows // 2)
    bottom = slice(rows // 2, rows)
    cw = [(i, (i + 1) % 4) for i in range(4)]
    ccw = [(i, (i - 1) % 4) for i in range(4)]
    opposite = pick(block, 1, (x + 2) % 4)
    from_left = lax.ppermute(opposite[top].astype(jnp.bfloat16), "x", cw).astype(jnp.float32)
    from_right = lax.ppermute(opposite[bottom].astype(jnp.bfloat16), "x", ccw).astype(
        jnp.float32
    )
    right = pick(block, 1, (x + 1) % 4)
    left = pick(block, 1, (x - 1) % 4)
    own = pick(block, 1, x)

    def second_round(sub):
        to_right = jnp.concatenate(
            [pick(right, 1, sub)[top] + pick(from_left, 1, sub), pick(right, 1, sub)[bottom]]
        )
        to_left = jnp.concatenate(
            [pick(left, 1, sub)[top], pick(left, 1, sub)[bottom] + pick(from_right, 1, sub)]
        )
        got_left = lax.ppermute(to_right.astype(jnp.bfloat16), "x", cw)
        got_right = lax.ppermute(to_left.astype(jnp.bfloat16), "x", ccw)
        return pick(own, 1, sub) + got_left.astype(jnp.float32) + got_right.astype(jnp.float32)

    sent = second_round(1 - zh).astype(jnp.bfloat16)
    got = lax.ppermute(sent, "zh", [(0, 1), (1, 0)])
    kept = second_round(zh)
    return kept + got.astype(jnp.float32)


def reduce_scatter(sums):
    zh = lax.axis_index("zh")
    n_x, n_zh = sums.shape[2], sums.shape[1]
    if n_x == 4 and n_zh == 2:
        return four_then_pair(jnp.swapaxes(sums, 1, 2))
    if n_x == 4:
        sums = four_scatter(jnp.swapaxes(sums, 1, 2))
    elif n_x > 1:
        sums = jnp.stack([ring_scatter(sums[:, z], 1, n_x) for z in range(n_zh)], axis=1)
    else:
        sums = sums[:, :, 0]
    if n_zh > 1:
        route = [(i, (i + 1) % n_zh) for i in range(n_zh)]
        acc = pick(sums, 1, (zh - 1) % n_zh)
        for k in range(1, n_zh):
            got = lax.ppermute(acc.astype(jnp.bfloat16), "zh", route)
            acc = got.astype(jnp.float32) + pick(sums, 1, (zh - 1 - k) % n_zh)
        return acc
    return sums[:, 0]


def attention_kernel(q_ref, do_ref, o_ref, k_ref, v_ref, mask_ref, dq_ref, dk_ref, dv_ref):
    tile_at = pl.program_id(0)
    score_scale = HD ** (-0.5)
    queries = q_ref[...]
    grads = do_ref[...]
    keys = k_ref[...]
    values = v_ref[...]
    live = mask_ref[0] > 0.0
    contract_last = (((1,), (1,)), ((), ()))
    contract_first = (((0,), (0,)), ((), ()))
    scores = lax.dot_general(queries, keys, contract_last, preferred_element_type=jnp.float32)
    scores = jnp.where(live, scores * score_scale, -jnp.inf)
    row_peak = jnp.max(scores, axis=1, keepdims=True)
    raised = jnp.where(live, jnp.exp(scores - row_peak), 0.0)
    row_total = jnp.sum(raised, axis=1, keepdims=True)
    weights = (raised / row_total).astype(jnp.bfloat16)
    delta = jnp.sum(
        grads.astype(jnp.float32) * o_ref[...].astype(jnp.float32), axis=1, keepdims=True
    )
    prob_grad = lax.dot_general(grads, values, contract_last, preferred_element_type=jnp.float32)
    score_grad = (weights.astype(jnp.float32) * (prob_grad - delta) * score_scale).astype(
        jnp.bfloat16
    )
    dq_ref[...] = jnp.dot(score_grad, keys, preferred_element_type=jnp.float32).astype(
        dq_ref.dtype
    )
    key_part = lax.dot_general(score_grad, queries, contract_first, preferred_element_type=jnp.float32)
    value_part = lax.dot_general(weights, grads, contract_first, preferred_element_type=jnp.float32)

    @pl.when(tile_at == 0)
    def _():
        dk_ref[...] = key_part
        dv_ref[...] = value_part

    @pl.when(tile_at > 0)
    def _():
        dk_ref[...] += key_part
        dv_ref[...] += value_part


def attention(queries, grads, outputs, keys, values, mask):
    rows = queries.shape[0]
    keys_n = keys.shape[0]
    tiles = rows // TILE
    row_spec = pl.BlockSpec((TILE, HD), lambda t: (t, 0))
    whole = pl.BlockSpec((keys_n, HD), lambda t: (0, 0))
    flops = 10 * rows * keys_n * HD
    return pl.pallas_call(
        attention_kernel,
        grid=(tiles,),
        in_specs=[
            row_spec,
            row_spec,
            row_spec,
            whole,
            whole,
            pl.BlockSpec((1, 1, keys_n), lambda t: (t, 0, 0)),
        ],
        out_specs=[row_spec, whole, whole],
        out_shape=[
            jax.ShapeDtypeStruct((rows, HD), jnp.bfloat16),
            jax.ShapeDtypeStruct((keys_n, HD), jnp.float32),
            jax.ShapeDtypeStruct((keys_n, HD), jnp.float32),
        ],
        compiler_params=pltpu.CompilerParams(
            dimension_semantics=("arbitrary",), vmem_limit_bytes=48 * 1024 * 1024
        ),
        cost_estimate=pl.CostEstimate(
            flops=flops,
            transcendentals=rows * keys_n,
            bytes_accessed=2 * (3 * rows * HD + 2 * keys_n * HD) + 8 * keys_n * HD,
        ),
    )(queries, grads, outputs, keys, values, mask)


def local(
    query_rows, key_rows, value_rows, output_rows, output_grad, projection, neighbours, counts
):
    seq_count = lax.axis_size("seq")
    place = lax.axis_index("seq")
    rows_dev = query_rows.shape[0]
    tiles_dev = rows_dev // TILE
    tiles_all = tiles_dev * seq_count
    heads_dev = query_rows.shape[1] // HD
    win = 3 * tiles_dev
    score_scale = HD ** (-0.5)
    first_tile = (place - 1) * tiles_dev
    window = with_halo(jnp.stack([key_rows, value_rows]), "seq", rows_dev)
    key_window = window[0].reshape(win * TILE, heads_dev, HD)
    value_window = window[1].reshape(win * TILE, heads_dev, HD)
    slot_range = jnp.arange(NB)
    window_ids = jnp.arange(win)
    masks = []
    for tile_at in range(tiles_dev):
        global_tile = place * tiles_dev + tile_at
        listed = neighbours[global_tile]
        is_live = slot_range < counts[global_tile]
        slots = (listed - first_tile) % tiles_all
        used = jnp.any((slots[:, None] == window_ids[None, :]) & is_live[:, None], axis=0)
        masks.append(jnp.repeat(used, TILE).astype(jnp.float32))
    mask = jnp.stack(masks)[:, None, :]
    query_grads, key_accs, value_accs = [], [], []
    for head_at in range(heads_dev):
        cols = slice(head_at * HD, (head_at + 1) * HD)
        dq, dk, dv = attention(
            query_rows[:, cols],
            output_grad[:, cols],
            output_rows[:, cols],
            key_window[:, head_at],
            value_window[:, head_at],
            mask,
        )
        query_grads.append(dq)
        key_accs.append(dk)
        value_accs.append(dv)
    key_acc = jnp.stack(key_accs, axis=1)
    value_acc = jnp.stack(value_accs, axis=1)
    partials = jnp.stack([key_acc, value_acc])
    from_next = passed_along(partials[:, :rows_dev].astype(jnp.bfloat16), "seq", -1).astype(
        jnp.float32
    )
    from_prev = passed_along(
        partials[:, 2 * rows_dev :].astype(jnp.bfloat16), "seq", 1
    ).astype(jnp.float32)
    owned = partials[:, rows_dev : 2 * rows_dev] + from_next + from_prev
    key_grads = owned[0].astype(jnp.bfloat16).reshape(rows_dev, heads_dev * HD)
    value_grads = owned[1].astype(jnp.bfloat16).reshape(rows_dev, heads_dev * HD)
    grad_stack = jnp.stack(
        [jnp.concatenate(query_grads, axis=1), key_grads, value_grads]
    )
    n_zh, n_x, n_c = (lax.axis_size(a) for a in HEAD_AXES)
    width = projection.shape[2] // (n_zh * n_x * n_c)
    weight = projection.reshape(3, heads_dev * HD, n_zh, n_x, n_c, width)
    c = lax.axis_index("c")

    def term(columns):
        return jnp.einsum("cik,ckzxm->izxm", grad_stack, columns, preferred_element_type=jnp.float32)

    if n_c > 1:
        other = term(pick(weight, 4, 1 - c)).astype(jnp.bfloat16)
        got = lax.ppermute(other, "c", [(0, 1), (1, 0)])
        mine = term(pick(weight, 4, c)).astype(jnp.bfloat16)
        sums = mine.astype(jnp.float32) + got.astype(jnp.float32)
    else:
        sums = term(weight[:, :, :, :, 0]).astype(jnp.bfloat16).astype(jnp.float32)
    return reduce_scatter(sums).astype(jnp.bfloat16)


def head_shape(n_head):
    n_c = 2 if n_head % 2 == 0 else 1
    n_x = 4 if (n_head // n_c) % 4 == 0 else n_head // n_c
    return n_head // (n_c * n_x), n_x, n_c


def solution(mesh):
    n_seq, n_head = mesh.devices.shape
    split = Mesh(mesh.devices.reshape((n_seq,) + head_shape(n_head)), ("seq",) + HEAD_AXES)
    rows = P("seq", HEAD_AXES)
    in_specs = (rows, rows, rows, rows, rows, P(None, HEAD_AXES, None), P(), P())
    return jax.shard_map(local, mesh=split, in_specs=in_specs, out_specs=rows, check_vma=False)
```

```python
import jax
import jax.numpy as jnp
from jax import lax
from jax.experimental import pallas as pl
from jax.experimental.pallas import tpu as pltpu
from jax.sharding import Mesh
from jax.sharding import PartitionSpec as P

HD = 128
TILE = 384
NB = 4
HEAD_AXES = ("zh", "x", "c")


def with_halo(cells, axis, width):
    count = lax.axis_size(axis)
    head = lax.slice_in_dim(cells, 0, width, axis=1)
    tail = lax.slice_in_dim(cells, cells.shape[1] - width, cells.shape[1], axis=1)
    return jnp.concatenate(
        [
            lax.ppermute(tail, axis, [(i, (i + 1) % count) for i in range(count)]),
            cells,
            lax.ppermute(head, axis, [((i + 1) % count, i) for i in range(count)]),
        ],
        axis=1,
    )


def passed_along(block, axis, distance):
    devices = range(lax.axis_size(axis))
    route = [((i - distance) % len(devices), i) for i in devices]
    return lax.ppermute(block, axis, route)


def pick(array, axis, index):
    return lax.dynamic_index_in_dim(array, index, axis, keepdims=False)


def ring_scatter(block, route_sign, n_x):
    x = lax.axis_index("x")
    rows = block.shape[0]
    halves = [block[: rows // 2], block[rows // 2 :]]
    out = []
    for h, half in enumerate(halves):
        step = route_sign if h == 0 else -route_sign
        route = [(i, (i + step) % n_x) for i in range(n_x)]
        acc = pick(half, 1, (x - step) % n_x)
        for k in range(1, n_x):
            got = lax.ppermute(acc.astype(jnp.bfloat16), "x", route)
            acc = got.astype(jnp.float32) + pick(half, 1, (x - step * (1 + k)) % n_x)
        out.append(acc)
    return jnp.concatenate(out, axis=0)


def four_scatter(block):
    x = lax.axis_index("x")
    rows = block.shape[0]
    top = slice(0, rows // 2)
    bottom = slice(rows // 2, rows)
    cw = [(i, (i + 1) % 4) for i in range(4)]
    ccw = [(i, (i - 1) % 4) for i in range(4)]
    opposite = pick(block, 1, (x + 2) % 4)
    from_left = lax.ppermute(opposite[top].astype(jnp.bfloat16), "x", cw)
    from_right = lax.ppermute(opposite[bottom].astype(jnp.bfloat16), "x", ccw)
    right = pick(block, 1, (x + 1) % 4)
    left = pick(block, 1, (x - 1) % 4)
    to_right = jnp.concatenate([right[top] + from_left.astype(jnp.float32), right[bottom]])
    to_left = jnp.concatenate([left[top], left[bottom] + from_right.astype(jnp.float32)])
    got_left = lax.ppermute(to_right.astype(jnp.bfloat16), "x", cw)
    got_right = lax.ppermute(to_left.astype(jnp.bfloat16), "x", ccw)
    return pick(block, 1, x) + got_left.astype(jnp.float32) + got_right.astype(jnp.float32)


def reduce_scatter(sums):
    zh = lax.axis_index("zh")
    n_x, n_zh = sums.shape[2], sums.shape[1]
    if n_x == 4:
        sums = four_scatter(jnp.swapaxes(sums, 1, 2))
    elif n_x > 1:
        sums = jnp.stack([ring_scatter(sums[:, z], 1, n_x) for z in range(n_zh)], axis=1)
    else:
        sums = sums[:, :, 0]
    if n_zh > 1:
        route = [(i, (i + 1) % n_zh) for i in range(n_zh)]
        acc = pick(sums, 1, (zh - 1) % n_zh)
        for k in range(1, n_zh):
            got = lax.ppermute(acc.astype(jnp.bfloat16), "zh", route)
            acc = got.astype(jnp.float32) + pick(sums, 1, (zh - 1 - k) % n_zh)
        return acc
    return sums[:, 0]


def attention_kernel(q_ref, do_ref, o_ref, k_ref, v_ref, mask_ref, dq_ref, dk_ref, dv_ref):
    tile_at = pl.program_id(0)
    score_scale = HD ** (-0.5)
    queries = q_ref[...]
    grads = do_ref[...]
    keys = k_ref[...]
    values = v_ref[...]
    live = mask_ref[0] > 0.0
    contract_last = (((1,), (1,)), ((), ()))
    contract_first = (((0,), (0,)), ((), ()))
    scores = lax.dot_general(queries, keys, contract_last, preferred_element_type=jnp.float32)
    scores = jnp.where(live, scores * score_scale, -jnp.inf)
    row_peak = jnp.max(scores, axis=1, keepdims=True)
    raised = jnp.where(live, jnp.exp(scores - row_peak), 0.0)
    row_total = jnp.sum(raised, axis=1, keepdims=True)
    weights = (raised / row_total).astype(jnp.bfloat16)
    delta = jnp.sum(
        grads.astype(jnp.float32) * o_ref[...].astype(jnp.float32), axis=1, keepdims=True
    )
    prob_grad = lax.dot_general(grads, values, contract_last, preferred_element_type=jnp.float32)
    score_grad = (weights.astype(jnp.float32) * (prob_grad - delta) * score_scale).astype(
        jnp.bfloat16
    )
    dq_ref[...] = jnp.dot(score_grad, keys, preferred_element_type=jnp.float32).astype(
        dq_ref.dtype
    )
    key_part = lax.dot_general(score_grad, queries, contract_first, preferred_element_type=jnp.float32)
    value_part = lax.dot_general(weights, grads, contract_first, preferred_element_type=jnp.float32)

    @pl.when(tile_at == 0)
    def _():
        dk_ref[...] = key_part
        dv_ref[...] = value_part

    @pl.when(tile_at > 0)
    def _():
        dk_ref[...] += key_part
        dv_ref[...] += value_part


def attention(queries, grads, outputs, keys, values, mask):
    rows = queries.shape[0]
    keys_n = keys.shape[0]
    tiles = rows // TILE
    row_spec = pl.BlockSpec((TILE, HD), lambda t: (t, 0))
    whole = pl.BlockSpec((keys_n, HD), lambda t: (0, 0))
    flops = 10 * rows * keys_n * HD
    return pl.pallas_call(
        attention_kernel,
        grid=(tiles,),
        in_specs=[
            row_spec,
            row_spec,
            row_spec,
            whole,
            whole,
            pl.BlockSpec((1, 1, keys_n), lambda t: (t, 0, 0)),
        ],
        out_specs=[row_spec, whole, whole],
        out_shape=[
            jax.ShapeDtypeStruct((rows, HD), jnp.bfloat16),
            jax.ShapeDtypeStruct((keys_n, HD), jnp.float32),
            jax.ShapeDtypeStruct((keys_n, HD), jnp.float32),
        ],
        compiler_params=pltpu.CompilerParams(
            dimension_semantics=("arbitrary",), vmem_limit_bytes=48 * 1024 * 1024
        ),
        cost_estimate=pl.CostEstimate(
            flops=flops,
            transcendentals=rows * keys_n,
            bytes_accessed=2 * (3 * rows * HD + 2 * keys_n * HD) + 8 * keys_n * HD,
        ),
    )(queries, grads, outputs, keys, values, mask)


def local(
    query_rows, key_rows, value_rows, output_rows, output_grad, projection, neighbours, counts
):
    seq_count = lax.axis_size("seq")
    place = lax.axis_index("seq")
    rows_dev = query_rows.shape[0]
    tiles_dev = rows_dev // TILE
    tiles_all = tiles_dev * seq_count
    heads_dev = query_rows.shape[1] // HD
    win = 3 * tiles_dev
    score_scale = HD ** (-0.5)
    first_tile = (place - 1) * tiles_dev
    window = with_halo(jnp.stack([key_rows, value_rows]), "seq", rows_dev)
    key_window = window[0].reshape(win * TILE, heads_dev, HD)
    value_window = window[1].reshape(win * TILE, heads_dev, HD)
    slot_range = jnp.arange(NB)
    window_ids = jnp.arange(win)
    masks = []
    for tile_at in range(tiles_dev):
        global_tile = place * tiles_dev + tile_at
        listed = neighbours[global_tile]
        is_live = slot_range < counts[global_tile]
        slots = (listed - first_tile) % tiles_all
        used = jnp.any((slots[:, None] == window_ids[None, :]) & is_live[:, None], axis=0)
        masks.append(jnp.repeat(used, TILE).astype(jnp.float32))
    mask = jnp.stack(masks)[:, None, :]
    query_grads, key_accs, value_accs = [], [], []
    for head_at in range(heads_dev):
        cols = slice(head_at * HD, (head_at + 1) * HD)
        dq, dk, dv = attention(
            query_rows[:, cols],
            output_grad[:, cols],
            output_rows[:, cols],
            key_window[:, head_at],
            value_window[:, head_at],
            mask,
        )
        query_grads.append(dq)
        key_accs.append(dk)
        value_accs.append(dv)
    key_acc = jnp.stack(key_accs, axis=1)
    value_acc = jnp.stack(value_accs, axis=1)
    partials = jnp.stack([key_acc, value_acc])
    from_next = passed_along(partials[:, :rows_dev].astype(jnp.bfloat16), "seq", -1).astype(
        jnp.float32
    )
    from_prev = passed_along(
        partials[:, 2 * rows_dev :].astype(jnp.bfloat16), "seq", 1
    ).astype(jnp.float32)
    owned = partials[:, rows_dev : 2 * rows_dev] + from_next + from_prev
    key_grads = owned[0].astype(jnp.bfloat16).reshape(rows_dev, heads_dev * HD)
    value_grads = owned[1].astype(jnp.bfloat16).reshape(rows_dev, heads_dev * HD)
    grad_stack = jnp.stack(
        [jnp.concatenate(query_grads, axis=1), key_grads, value_grads]
    )
    n_zh, n_x, n_c = (lax.axis_size(a) for a in HEAD_AXES)
    width = projection.shape[2] // (n_zh * n_x * n_c)
    weight = projection.reshape(3, heads_dev * HD, n_zh, n_x, n_c, width)
    c = lax.axis_index("c")

    def term(columns):
        return jnp.einsum("cik,ckzxm->izxm", grad_stack, columns, preferred_element_type=jnp.float32)

    if n_c > 1:
        other = term(pick(weight, 4, 1 - c)).astype(jnp.bfloat16)
        got = lax.ppermute(other, "c", [(0, 1), (1, 0)])
        mine = term(pick(weight, 4, c)).astype(jnp.bfloat16)
        mine, got = lax.optimization_barrier((mine, got))
        sums = mine.astype(jnp.float32) + got.astype(jnp.float32)
    else:
        sums = term(weight[:, :, :, :, 0]).astype(jnp.bfloat16).astype(jnp.float32)
    return reduce_scatter(sums).astype(jnp.bfloat16)


def head_shape(n_head):
    n_c = 2 if n_head % 2 == 0 else 1
    n_x = 4 if (n_head // n_c) % 4 == 0 else n_head // n_c
    return n_head // (n_c * n_x), n_x, n_c


def solution(mesh):
    n_seq, n_head = mesh.devices.shape
    split = Mesh(mesh.devices.reshape((n_seq,) + head_shape(n_head)), ("seq",) + HEAD_AXES)
    rows = P("seq", HEAD_AXES)
    in_specs = (rows, rows, rows, rows, rows, P(None, HEAD_AXES, None), P(), P())
    return jax.shard_map(local, mesh=split, in_specs=in_specs, out_specs=rows, check_vma=False)
```
